512 devices in a mesh: rep: 16 (over z), ctx: 32 (over x, y, core).
Axes of the slice: x: 4, y: 4, z: 16, core: 2. Of those that a mesh axis runs over, the one named last changes fastest.
Arguments:
- query_rows: bfloat16 [16, 4096, 32, 128], P('rep', 'ctx'), may hold values from -17 to 17
- key_rows: bfloat16 [16, 4096, 4, 128], P('rep', 'ctx'), may hold values from -17 to 17
- value_matrix: bfloat16 [16, 4096, 4, 128], P('rep', 'ctx'), may hold values from -6 to 6
- cotangent: bfloat16 [16, 4096, 32, 128], P('rep', 'ctx'), may hold values from -6 to 6
- rotation: bfloat16 [16, 4, 32, 128], replicated, may hold values from -0.29882812 to 0.29882812
- projection: bfloat16 [16, 4, 32, 128], replicated, may hold values from -0.29882812 to 0.29882812
- shift_bias: float32 [16, 4], replicated, may hold values from -4 to 4
- doc_starts: int32 [16, 4096], P('rep'), may hold values from 0 to 4094, as said below
- tenant_ids: int32 [16, 4096], P('rep'), may hold values from 0 to 15, as said below
Outputs:
- d_queries: bfloat16 [16, 4096, 32, 128], P('rep', 'ctx')
- d_keys: bfloat16 [16, 4096, 4, 128], P('rep', 'ctx')
- d_values: bfloat16 [16, 4096, 4, 128], P('rep', 'ctx')
- grad_rotation: float32 [16, 4, 32, 128], P('rep', None, 'ctx')
- grad_projection: float32 [16, 4, 32, 128], P('rep', None, 'ctx')
The draws below stay inside these ranges and needn't reach their ends.
Inputs may be any that keep to these rules, and one draw needn't show every extreme that they name: doc_starts[r, i] is the first position of the document holding position i of sequence r; documents are consecutive, each of even length 2 to 256; every sequence begins with one of exactly 256 and ends with one of length 2. `tenant_ids`: the tenant of a position's document: equal for all positions of one document.
All inputs are finite; a program needn't handle non-finite values.
Results may differ from the reference program's by a relative error of at most 0.03.
Values may be sent and summed in bfloat16 or wider, within the bound.
A program may use at most 128 MiB of HBM per device.

```python
import jax
import jax.numpy as jnp
from jax import lax

QUERY_HEADS = 32
KEY_VALUE_HEADS = 4
HEAD_SIZE = 128
RANK = 4
TEN = 16
DOC_MAX = 256
BLK = 512
SEQUENCE_COUNT = 16
SEQUENCE_LENGTH = 4096


def doc_layout(key):
    base_key = jax.random.fold_in(key, 101)
    key_length, key_tenant = jax.random.split(base_key)
    half_len = SEQUENCE_LENGTH // 2
    increments = 2 * jax.random.randint(key_length, (SEQUENCE_COUNT, half_len), 1, DOC_MAX // 2 + 1)
    increments = increments.at[:, 0].set(DOC_MAX)
    bounds = jnp.concatenate([jnp.zeros((SEQUENCE_COUNT, 1), jnp.int32), jnp.cumsum(increments, axis=1).astype(jnp.int32)], axis=1)
    positions = jnp.arange(SEQUENCE_LENGTH, dtype=jnp.int32)
    doc_slot = jax.vmap(lambda bound_row: jnp.searchsorted(bound_row, positions, side='right'))(bounds) - 1
    starts = jnp.take_along_axis(bounds, doc_slot, axis=1)
    tail_mask = positions[None, :] >= SEQUENCE_LENGTH - 2
    starts = jnp.where(tail_mask, SEQUENCE_LENGTH - 2, starts)
    doc_slot = jnp.where(tail_mask, half_len + 1, doc_slot)
    tenant_table = jax.random.randint(key_tenant, (SEQUENCE_COUNT, half_len + 2), 0, TEN)
    tenant_table = tenant_table.at[:, 0].set(TEN - 1).at[:, 1].set(0)
    tenants = jnp.take_along_axis(tenant_table, doc_slot, axis=1)
    return (starts.astype(jnp.int32), tenants.astype(jnp.int32))


def draw_doc_starts(key, part):
    return doc_layout(key)[0]


def draw_tenant_ids(key, part):
    return doc_layout(key)[1]


def draw_query_rows(key, part):
    array_shape = (SEQUENCE_COUNT, SEQUENCE_LENGTH, QUERY_HEADS, HEAD_SIZE)
    values = jax.random.truncated_normal(jax.random.fold_in(key, 1), -4.0, 4.0, array_shape, jnp.float32)
    return values.astype(jnp.bfloat16)


def draw_key_rows(key, part):
    array_shape = (SEQUENCE_COUNT, SEQUENCE_LENGTH, KEY_VALUE_HEADS, HEAD_SIZE)
    values = jax.random.truncated_normal(jax.random.fold_in(key, 2), -4.0, 4.0, array_shape, jnp.float32)
    return values.astype(jnp.bfloat16)


def steps_of(stream_key, shape, cuts, least, high):
    loudness = 1.0
    for axis_at, parts in cuts:
        steps = jax.random.uniform(jax.random.fold_in(jax.random.fold_in(stream_key, 6), axis_at), (parts,), jnp.float32, least / len(cuts), high / len(cuts))
        loudness = loudness * jnp.repeat(jnp.exp(steps), shape[axis_at] // parts).reshape((-1,) + (1,) * (len(shape) - 1 - axis_at))
    return loudness


def bell_draw(rng, extent, spread, reach, cuts=(), kind=jnp.bfloat16):
    drawn = jax.random.normal(rng, extent, jnp.float32) * spread
    if len(cuts) > 0:
        drawn = steps_of(rng, extent, cuts, -0.22, 0.18) * drawn
    return jnp.clip(drawn, min=-reach, max=reach).astype(kind)


def setup_inputs(seed: int = 0) -> dict:
    keys = jax.random.split(jax.random.key(seed), 10)
    return {
        "query_rows": draw_query_rows(jax.random.fold_in(keys[9], 71), 0),
        "key_rows": draw_key_rows(jax.random.fold_in(keys[9], 71), 0),
        "value_matrix": bell_draw(keys[2], (SEQUENCE_COUNT, SEQUENCE_LENGTH, KEY_VALUE_HEADS, HEAD_SIZE), 1.0, 6.0, ((0, 16), (1, 32))),
        "cotangent": bell_draw(keys[3], (SEQUENCE_COUNT, SEQUENCE_LENGTH, QUERY_HEADS, HEAD_SIZE), 1.0, 6.0, ((0, 16), (1, 32))),
        "rotation": bell_draw(keys[4], (TEN, RANK, QUERY_HEADS, HEAD_SIZE), 0.05, 0.29882812),
        "projection": bell_draw(keys[5], (TEN, RANK, QUERY_HEADS, HEAD_SIZE), 0.05, 0.29882812),
        "shift_bias": bell_draw(keys[6], (TEN, RANK), 1.0, 4.0, (), jnp.float32),
        "doc_starts": draw_doc_starts(jax.random.fold_in(keys[9], 71), 0),
        "tenant_ids": draw_tenant_ids(jax.random.fold_in(keys[9], 71), 0),
    }


far_below = -1e30


def masked_scores(query_block, key_window, start_block, row_start):
    scaling = query_block.shape[-1] ** -0.5
    scores = jnp.einsum("qhd,khd->hqk", query_block.astype(jnp.float32), key_window.astype(jnp.float32)) * scaling
    query_place = row_start + jnp.arange(query_block.shape[0], dtype=jnp.int32)
    key_place = row_start + query_block.shape[0] - key_window.shape[0] + jnp.arange(key_window.shape[0], dtype=jnp.int32)
    allowed = (key_place[None, :] >= start_block[:, None]) & (key_place[None, :] <= query_place[:, None])
    return jnp.where(allowed[None], scores, far_below)


def one_sequence(queries, key_set, value_set, upstream, starts, owners, rotation, projection, shift_bias):
    head_count = queries.shape[1]
    kv_count = key_set.shape[1]
    group_size = head_count // kv_count
    head_dim = queries.shape[2]
    length = queries.shape[0]
    scaling = head_dim ** -0.5
    spread_keys = jnp.repeat(key_set, group_size, axis=1)
    spread_values = jnp.repeat(value_set, group_size, axis=1)
    padding = jnp.zeros((DOC_MAX, head_count, head_dim), jnp.bfloat16)
    padded_keys = jnp.concatenate([padding, spread_keys], axis=0)
    padded_values = jnp.concatenate([padding, spread_values], axis=0)
    window = BLK + DOC_MAX
    block_count = length // BLK

    def windows(block_index):
        row_start = block_index * BLK
        return (row_start,
                lax.dynamic_slice_in_dim(queries, row_start, BLK, 0),
                lax.dynamic_slice_in_dim(padded_keys, row_start, window, 0),
                lax.dynamic_slice_in_dim(padded_values, row_start, window, 0),
                lax.dynamic_slice_in_dim(starts, row_start, BLK, 0))

    def forward_block(running, block_index):
        row_start, query_block, key_window, value_window, start_block = windows(block_index)
        scores = masked_scores(query_block, key_window, start_block, row_start)
        row_max = jnp.max(scores, axis=-1)
        weights = jnp.exp(scores - row_max[..., None])
        row_total = jnp.sum(weights, axis=-1)
        weights_low = (weights / row_total[..., None]).astype(jnp.bfloat16)
        outputs = jnp.einsum("hqk,khd->qhd", weights_low.astype(jnp.float32), value_window.astype(jnp.float32)).astype(jnp.bfloat16)
        return running, (row_max, row_total, outputs)

    block_ids = jnp.arange(block_count, dtype=jnp.int32)
    _, (maxima, totals, outputs) = lax.scan(forward_block, jnp.zeros((), jnp.int32), block_ids)
    hidden = outputs.reshape(length, head_count, head_dim)

    tenant_mask = (jnp.arange(rotation.shape[0], dtype=jnp.int32)[:, None] == owners[None, :]).astype(jnp.float32)
    hidden_wide = hidden.astype(jnp.float32)
    upstream_wide = upstream.astype(jnp.float32)
    projection_wide = projection.astype(jnp.float32)
    rotation_wide = rotation.astype(jnp.float32)
    on_projection = jnp.einsum("shd,trhd->trs", hidden_wide, projection_wide)
    on_rotation = jnp.einsum("shd,trhd->trs", hidden_wide, rotation_wide)
    pulled_all = jnp.einsum("shd,trhd->trs", upstream_wide, rotation_wide)
    bias_rows = jnp.sum(shift_bias[:, :, None] * tenant_mask[:, None, :], axis=0)
    lifted = jnp.sum(on_projection * tenant_mask[:, None, :], axis=0) - jnp.sum(on_rotation * tenant_mask[:, None, :], axis=0) + bias_rows
    pulled = jnp.sum(pulled_all * tenant_mask[:, None, :], axis=0)
    lifted_low = lifted.astype(jnp.bfloat16)
    pulled_low = pulled.astype(jnp.bfloat16)
    picked_pull = tenant_mask[:, None, :] * pulled_low.astype(jnp.float32)[None]
    picked_lift = tenant_mask[:, None, :] * lifted_low.astype(jnp.float32)[None]
    grad_projection = jnp.einsum("trs,shd->trhd", picked_pull, hidden_wide)
    grad_rotation = jnp.einsum("trs,shd->trhd", picked_lift, upstream_wide) - grad_projection
    hidden_grad = upstream_wide + jnp.einsum("trs,trhd->shd", picked_pull, projection_wide) - jnp.einsum("trs,trhd->shd", picked_pull, rotation_wide)
    grad_hidden = hidden_grad.astype(jnp.bfloat16)
    row_delta = jnp.sum(grad_hidden.astype(jnp.float32) * hidden_wide, axis=-1)

    def backward_block(running, pieces):
        block_index, row_max, row_total = pieces
        key_total, value_total = running
        row_start, query_block, key_window, value_window, start_block = windows(block_index)
        scores = masked_scores(query_block, key_window, start_block, row_start)
        weights = jnp.exp(scores - row_max[..., None]) / row_total[..., None]
        weights_low = weights.astype(jnp.bfloat16)
        grad_block = lax.dynamic_slice_in_dim(grad_hidden, row_start, BLK, 0).astype(jnp.float32)
        delta_block = lax.dynamic_slice_in_dim(row_delta, row_start, BLK, 0)
        value_grad = jnp.einsum("hqk,qhd->khd", weights_low.astype(jnp.float32), grad_block)
        weight_grad = jnp.einsum("qhd,khd->hqk", grad_block, value_window.astype(jnp.float32))
        score_grad = (weights * (weight_grad - delta_block.T[:, :, None])).astype(jnp.bfloat16).astype(jnp.float32)
        query_grad = jnp.einsum("hqk,khd->qhd", score_grad, key_window.astype(jnp.float32)) * scaling
        key_grad = jnp.einsum("hqk,qhd->khd", score_grad, query_block.astype(jnp.float32)) * scaling
        key_total = lax.dynamic_update_slice_in_dim(key_total, lax.dynamic_slice_in_dim(key_total, row_start, window, 0) + key_grad, row_start, 0)
        value_total = lax.dynamic_update_slice_in_dim(value_total, lax.dynamic_slice_in_dim(value_total, row_start, window, 0) + value_grad, row_start, 0)
        return (key_total, value_total), query_grad.astype(jnp.bfloat16)

    empty_total = jnp.zeros((length + DOC_MAX, head_count, head_dim), jnp.float32)
    (key_total, value_total), query_grads = lax.scan(backward_block, (empty_total, empty_total), (block_ids, maxima, totals))
    d_queries = query_grads.reshape(length, head_count, head_dim)
    head_dkeys = lax.optimization_barrier(key_total[DOC_MAX:].astype(jnp.bfloat16))
    head_dvalues = lax.optimization_barrier(value_total[DOC_MAX:].astype(jnp.bfloat16))
    d_keys = head_dkeys.astype(jnp.float32).reshape(length, kv_count, group_size, head_dim).sum(axis=2).astype(jnp.bfloat16)
    d_values = head_dvalues.astype(jnp.float32).reshape(length, kv_count, group_size, head_dim).sum(axis=2).astype(jnp.bfloat16)
    return d_queries, d_keys, d_values, grad_rotation, grad_projection


def reference(query_rows, key_rows, value_matrix, cotangent, rotation, projection, shift_bias, doc_starts, tenant_ids):
    def per_sequence(sequence):
        queries, key_set, value_set, upstream, starts, owners = sequence
        return one_sequence(queries, key_set, value_set, upstream, starts, owners, rotation, projection, shift_bias)

    d_queries, d_keys, d_values, grad_rotation, grad_projection = lax.map(
        per_sequence, (query_rows, key_rows, value_matrix, cotangent, doc_starts, tenant_ids))
    return d_queries, d_keys, d_values, jnp.sum(grad_rotation, axis=0), jnp.sum(grad_projection, axis=0)
```

```python
import jax
import jax.numpy as jnp
from jax import lax
from jax.experimental import pallas as pl
from jax.experimental.pallas import tpu as pltpu
from jax.sharding import PartitionSpec as P_

f32, bf16 = jnp.float32, jnp.bfloat16
MESH = pl.DeviceIdType.MESH
LOG2E = 1.4426950408889634


def dot(a, b):
    return jnp.dot(a, b, preferred_element_type=f32)


def dot_nt(a, b):
    return lax.dot_general(a, b, (((1,), (1,)), ((), ())), preferred_element_type=f32)


def iota(shape, d):
    return lax.broadcasted_iota(jnp.int32, shape, d)


def stage_prep(q_ref, c_ref, w_ref, r_ref, Q, C2, WR):
    for m in range(4):
        Q[m] = jnp.swapaxes(q_ref[:, 8 * m : 8 * m + 8, :], 0, 1).reshape(1024, 128)
    C2[...] = c_ref[...].reshape(128, 4096)
    WR[0:64] = w_ref[...].reshape(64, 4096)
    WR[64:128] = r_ref[...].reshape(64, 4096)


def stage_mask(starts, row_first, MB):
    key_place = row_first - 256 + iota((384, 128), 0)
    query_place = row_first + iota((384, 128), 1)
    allowed = (key_place >= starts) & (key_place <= query_place)
    MB[...] = jnp.where(allowed, 0.0, -1e30).astype(f32)


def stage_fwd(m, KV, Q, MB, P, HT, scale):
    vt = KV[m, 1].T
    st = dot_nt(KV[m, 0], Q[m])
    s = st * (scale * LOG2E) + jnp.concatenate([MB[...]] * 8, axis=1)
    e = jnp.exp2(s - jnp.max(s, axis=0, keepdims=True))
    wl = (e * (1.0 / jnp.sum(e, axis=0, keepdims=True))).astype(bf16)
    P[m] = wl
    ht = dot(vt, wl).astype(bf16)
    for g in range(8):
        HT[pl.ds(m * 1024 + g * 128, 128), :] = ht[:, g * 128 : (g + 1) * 128]


def stage_pull(own, WR, C2, GH, PL):
    mask = iota((64, 128), 0) // 4 == own
    pull = jnp.where(mask, dot_nt(WR[64:128], C2[...]), 0.0)
    PL[...] = pull.astype(bf16)
    pt = jnp.concatenate([pull, -pull], axis=0).T.astype(bf16)
    for m in range(4):
        cols = slice(m * 1024, (m + 1) * 1024)
        gh = (dot(pt, WR[:, cols]) + C2[:, cols].astype(f32)).astype(bf16)
        for g in range(8):
            GH[m, g * 128 : (g + 1) * 128, :] = gh[:, g * 128 : (g + 1) * 128]


def stage_tenant(own, bias_sm, WR, C2, HT, PL, G, send):
    mask = iota((64, 128), 0) // 4 == own
    lift2 = dot(WR[...], HT[...])
    ridx = iota((8, 128), 0)
    shifts = []
    for b in range(8):
        a = jnp.zeros((8, 128), f32)
        for r in range(8):
            a = jnp.where(ridx == r, bias_sm[(b * 8 + r) // 4, r % 4], a)
        shifts.append(a)
    lift = lift2[0:64] - lift2[64:128] + jnp.concatenate(shifts, axis=0)
    lift = jnp.where(mask, lift, 0.0).astype(bf16)
    r = iota((128, 64), 0)
    c = iota((128, 64), 1)
    hit = c == (r // 8) * 4 + r % 4
    first = (r // 4) % 2 == 0
    li = dot(jnp.where(hit & first, 1.0, 0.0).astype(bf16), lift).astype(bf16)
    pi = dot(jnp.where(hit, jnp.where(first, -1.0, 1.0), 0.0).astype(bf16), PL[...]).astype(bf16)
    for m in range(4):
        part = dot(li, C2[:, m * 1024 : (m + 1) * 1024])
        part = part + dot_nt(pi, HT[m * 1024 : (m + 1) * 1024, :])
        part = part.astype(bf16)
        for g in range(8):
            G[g % 2, m * 4 + g // 2] = part[:, g * 128 : (g + 1) * 128]
        send(m)


def stage_bwd(m, KV, Q, P, GH, scale, DQ, SB, OWN):
    kt = KV[m, 0].T
    gh = GH[m]
    dp = dot_nt(KV[m, 1], gh)
    wl = P[m]
    w = wl.astype(f32)
    wd = w * dp
    delta = jnp.sum(wd, axis=0, keepdims=True)
    ds = (wd - w * delta).astype(bf16)
    dk = dot(ds, Q[m]) * scale
    dv = dot(wl, gh)
    for s in (1, 2):
        rows = slice(HALO - 128 * s, HALO - 128 * s + 128)
        SB[m, s - 1, 0] = dk[rows].astype(bf16)
        SB[m, s - 1, 1] = dv[rows].astype(bf16)
    OWN[m, 0] = dk[HALO:]
    OWN[m, 1] = dv[HALO:]
    dqt = dot(kt, ds) * scale
    for g in range(8):
        DQ[m * 8 + g] = dqt[:, g * 128 : (g + 1) * 128].T.astype(bf16)


REPS, CTXS, CHIPS = 16, 32, 16
HALO = 256


def kernel(
    q_hbm, c_hbm, k_hbm, v_hbm, w_hbm, r_hbm, bias_sm, starts_ref, owners_ref,
    dq_ref, dk_ref, dv_ref, gr_ref, gp_ref,
    q_in, c_in, k_in, v_in, w_in, r_in, in_sem,
    KV, Q, C2, WR, MB, P, HT, GH, DQ, PL,
    halo_send, halo_recv,
    SB, RB, OWN, back_send, back_recv,
    G, R1, one_send, one_recv,
    S2, R2, two_send, two_recv,
    S3, R3, three_send, three_recv,
):
    rep = lax.axis_index("rep")
    ctx = lax.axis_index("ctx")
    chip = ctx // 2
    core = ctx % 2
    mate = ctx + 1 - 2 * core
    scale = 128 ** -0.5

    def there(x):
        return (rep, x)

    loads = []
    for i, (src, dst) in enumerate(
        ((k_hbm, k_in), (v_hbm, v_in), (q_hbm, q_in), (c_hbm, c_in), (w_hbm, w_in), (r_hbm, r_in))
    ):
        cp = pltpu.make_async_copy(src, dst, in_sem.at[i])
        cp.start()
        loads.append(cp)

    barrier = pltpu.get_barrier_semaphore()
    for d in (1, CTXS - 1):
        pl.semaphore_signal(barrier, inc=1, device_id=there((ctx + d) % CTXS), device_id_type=MESH)
    for d in range(1, CHIPS):
        pl.semaphore_signal(
            barrier, inc=1, device_id=there((ctx + 2 * d) % CTXS), device_id_type=MESH
        )
    for d in range(1, REPS):
        pl.semaphore_signal(
            barrier, inc=1, device_id=((rep + d) % REPS, ctx), device_id_type=MESH
        )

    loads[0].wait()
    loads[1].wait()
    kk = jnp.swapaxes(k_in[...].astype(f32), 0, 1).astype(bf16)
    vv = jnp.swapaxes(v_in[...].astype(f32), 0, 1).astype(bf16)
    for m in range(4):
        KV[m, 0, HALO:] = kk[m]
        KV[m, 1, HALO:] = vv[m]
    loads[2].wait()
    loads[3].wait()
    loads[4].wait()
    loads[5].wait()
    stage_prep(q_in, c_in, w_in, r_in, Q, C2, WR)
    row_first = ctx * 128
    lanes = pl.ds(pl.multiple_of(row_first, 128), 128)
    own = owners_ref[:, lanes]
    stage_mask(starts_ref[:, lanes], row_first, MB)

    pl.semaphore_wait(barrier, 2 + (CHIPS - 1) + (REPS - 1))

    def halo_copy(m, s):
        return pltpu.make_async_remote_copy(
            src_ref=KV.at[m, :, pl.ds(HALO, 128)],
            dst_ref=KV.at[m, :, pl.ds(HALO - 128 * s, 128)],
            send_sem=halo_send.at[m, s - 1],
            recv_sem=halo_recv.at[m, s - 1],
            device_id=there((ctx + s) % CTXS),
            device_id_type=MESH,
        )

    for m in range(4):
        for s in (1, 2):
            halo_copy(m, s).start()

    stage_pull(own, WR, C2, GH, PL)

    def fwd(m, carry):
        for s in (1, 2):
            halo_copy(m, s).wait_recv()
        stage_fwd(m, KV, Q, MB, P, HT, scale)
        return carry

    lax.fori_loop(0, 4, fwd, 0)

    def one_copy(m):
        return pltpu.make_async_remote_copy(
            src_ref=G.at[1 - core, pl.ds(4 * m, 4)],
            dst_ref=R1.at[pl.ds(4 * m, 4)],
            send_sem=one_send.at[m],
            recv_sem=one_recv.at[m],
            device_id=there(mate),
            device_id_type=MESH,
        )

    def two_copy(d):
        return pltpu.make_async_remote_copy(
            src_ref=S2.at[(chip + d) % CHIPS],
            dst_ref=R2.at[d],
            send_sem=two_send.at[d],
            recv_sem=two_recv.at[d],
            device_id=there((ctx + 2 * d) % CTXS),
            device_id_type=MESH,
        )

    def three_copy(d):
        return pltpu.make_async_remote_copy(
            src_ref=S3.at[(rep + d) % REPS],
            dst_ref=R3.at[d],
            send_sem=three_send.at[d],
            recv_sem=three_recv.at[d],
            device_id=((rep + d) % REPS, ctx),
            device_id_type=MESH,
        )

    def back_copy(m, s):
        return pltpu.make_async_remote_copy(
            src_ref=SB.at[m, s - 1],
            dst_ref=RB.at[m, s - 1],
            send_sem=back_send.at[m, s - 1],
            recv_sem=back_recv.at[m, s - 1],
            device_id=there((ctx + CTXS - s) % CTXS),
            device_id_type=MESH,
        )

    stage_tenant(own, bias_sm, WR, C2, HT, PL, G, lambda m: one_copy(m).start())

    def bwd(m, carry):
        stage_bwd(m, KV, Q, P, GH, scale, DQ, SB, OWN)
        for s in (1, 2):
            back_copy(m, s).start()

        @pl.when(m == 0)
        def _():
            for i in range(4):
                one_copy(i).wait_recv()
            S2[...] = (G[core].astype(f32) + R1[...].astype(f32)).astype(bf16)
            for d in range(1, CHIPS):
                two_copy(d).start()

        @pl.when(m == 2)
        def _():
            total = S2[chip].astype(f32)
            for d in range(1, CHIPS):
                two_copy(d).wait_recv()
                total = total + R2[d].astype(f32)
            S3[...] = total.reshape(REPS, 8, 128)
            for d in range(1, REPS):
                three_copy(d).start()

        return carry

    lax.fori_loop(0, 4, bwd, 0)

    for m in range(4):
        dq_ref[:, 8 * m : 8 * m + 8, :] = jnp.swapaxes(DQ[8 * m : 8 * m + 8], 0, 1)

    mine = S3[rep]
    for d in range(1, REPS):
        three_copy(d).wait_recv()
        mine = mine + R3[d]
    gr_ref[...] = mine[0:4]
    gp_ref[...] = mine[4:8]

    for m in range(4):
        for s in (1, 2):
            back_copy(m, s).wait_recv()
    total = OWN[...] + RB[:, 0].astype(f32) + RB[:, 1].astype(f32)
    dk_ref[...] = jnp.swapaxes(total[:, 0], 0, 1).astype(bf16)
    dv_ref[...] = jnp.swapaxes(total[:, 1], 0, 1).astype(bf16)

    for m in range(4):
        one_copy(m).wait_send()
        for s in (1, 2):
            halo_copy(m, s).wait_send()
            back_copy(m, s).wait_send()
    for d in range(1, CHIPS):
        two_copy(d).wait_send()
    for d in range(1, REPS):
        three_copy(d).wait_send()


def on_device(
    query_rows, key_rows, value_matrix, cotangent, rotation, projection, shift_bias,
    doc_starts, tenant_ids,
):
    vmem = pl.BlockSpec(memory_space=pltpu.VMEM)
    smem = pl.BlockSpec(memory_space=pltpu.SMEM)
    hbm = pl.BlockSpec(memory_space=pl.ANY)
    dma = pltpu.SemaphoreType.DMA
    rows = (128, 32, 128)
    out = pl.pallas_call(
        kernel,
        out_shape=(
            jax.ShapeDtypeStruct(rows, bf16),
            jax.ShapeDtypeStruct((128, 4, 128), bf16),
            jax.ShapeDtypeStruct((128, 4, 128), bf16),
            jax.ShapeDtypeStruct((4, 128), f32),
            jax.ShapeDtypeStruct((4, 128), f32),
        ),
        in_specs=[hbm] * 6 + [smem, vmem, vmem],
        out_specs=(vmem,) * 5,
        scratch_shapes=[
            pltpu.VMEM(rows, bf16), pltpu.VMEM(rows, bf16),
            pltpu.VMEM((128, 4, 128), bf16), pltpu.VMEM((128, 4, 128), bf16),
            pltpu.VMEM((64, 32, 128), bf16), pltpu.VMEM((64, 32, 128), bf16),
            dma((6,)),
            pltpu.VMEM((4, 2, 384, 128), bf16),
            pltpu.VMEM((4, 1024, 128), bf16),
            pltpu.VMEM((128, 4096), bf16),
            pltpu.VMEM((128, 4096), bf16),
            pltpu.VMEM((384, 128), f32),
            pltpu.VMEM((4, 384, 1024), bf16),
            pltpu.VMEM((4096, 128), bf16),
            pltpu.VMEM((4, 1024, 128), bf16),
            pltpu.VMEM((32, 128, 128), bf16),
            pltpu.VMEM((64, 128), bf16),
            dma((4, 2)), dma((4, 2)),
            pltpu.VMEM((4, 2, 2, 128, 128), bf16),
            pltpu.VMEM((4, 2, 2, 128, 128), bf16),
            pltpu.VMEM((4, 2, 128, 128), f32),
            dma((4, 2)), dma((4, 2)),
            pltpu.VMEM((2, CHIPS, 128, 128), bf16),
            pltpu.VMEM((CHIPS, 128, 128), bf16),
            dma((4,)), dma((4,)),
            pltpu.VMEM((CHIPS, 128, 128), bf16),
            pltpu.VMEM((CHIPS, 128, 128), bf16),
            dma((CHIPS,)), dma((CHIPS,)),
            pltpu.VMEM((REPS, 8, 128), f32),
            pltpu.VMEM((REPS, 8, 128), f32),
            dma((REPS,)), dma((REPS,)),
        ],
        compiler_params=pltpu.CompilerParams(
            collective_id=0, has_side_effects=True, vmem_limit_bytes=48 << 20
        ),
        name="steered_attention_backward",
    )(
        query_rows[0], cotangent[0], key_rows[0], value_matrix[0],
        projection.reshape(64, 32, 128), rotation.reshape(64, 32, 128),
        shift_bias, doc_starts, tenant_ids,
    )
    dq, dk, dv, gr, gp = out
    return dq[None], dk[None], dv[None], gr.reshape(1, 4, 1, 128), gp.reshape(1, 4, 1, 128)


def solution(mesh):
    row = P_("rep", "ctx", None, None)
    in_specs = (row, row, row, row, P_(), P_(), P_(), P_("rep", None), P_("rep", None))
    grads = P_("rep", None, "ctx", None)
    return jax.shard_map(
        on_device, mesh=mesh, in_specs=in_specs, out_specs=(row, row, row, grads, grads),
        check_vma=False,
    )
```

```python
import jax
import jax.numpy as jnp
from jax import lax
from jax.experimental import pallas as pl
from jax.experimental.pallas import tpu as pltpu
from jax.sharding import PartitionSpec as P_

f32, bf16 = jnp.float32, jnp.bfloat16
MESH = pl.DeviceIdType.MESH
LOG2E = 1.4426950408889634


def dot(a, b):
    return jnp.dot(a, b, preferred_element_type=f32)


def dot_nt(a, b):
    return lax.dot_general(a, b, (((1,), (1,)), ((), ())), preferred_element_type=f32)


def iota(shape, d):
    return lax.broadcasted_iota(jnp.int32, shape, d)


def stage_prep(q_ref, c_ref, w_ref, r_ref, Q, C2, WR):
    for m in range(4):
        Q[m] = jnp.swapaxes(q_ref[:, 8 * m : 8 * m + 8, :], 0, 1).reshape(1024, 128)
    C2[...] = c_ref[...].reshape(128, 4096)
    WR[0:64] = w_ref[...].reshape(64, 4096)
    WR[64:128] = r_ref[...].reshape(64, 4096)


def stage_mask(starts, row_first, MB):
    key_place = row_first - 256 + iota((384, 128), 0)
    query_place = row_first + iota((384, 128), 1)
    allowed = (key_place >= starts) & (key_place <= query_place)
    MB[...] = jnp.where(allowed, 0.0, -1e30).astype(f32)


def stage_fwd(m, KV, Q, MB, P, HT, scale):
    vt = KV[m, 1].T
    st = dot_nt(KV[m, 0], Q[m])
    s = st * (scale * LOG2E) + jnp.concatenate([MB[...]] * 8, axis=1)
    e = jnp.exp2(s - jnp.max(s, axis=0, keepdims=True))
    wl = (e * (1.0 / jnp.sum(e, axis=0, keepdims=True))).astype(bf16)
    P[m] = wl
    ht = dot(vt, wl).astype(bf16)
    for g in range(8):
        HT[pl.ds(m * 1024 + g * 128, 128), :] = ht[:, g * 128 : (g + 1) * 128]


def stage_pull(own, WR, C2, GH, PL):
    mask = iota((64, 128), 0) // 4 == own
    pull = jnp.where(mask, dot_nt(WR[64:128], C2[...]), 0.0)
    PL[...] = pull.astype(bf16)
    pt = jnp.concatenate([pull, -pull], axis=0).T.astype(bf16)
    for m in range(4):
        cols = slice(m * 1024, (m + 1) * 1024)
        gh = (dot(pt, WR[:, cols]) + C2[:, cols].astype(f32)).astype(bf16)
        for g in range(8):
            GH[m, g * 128 : (g + 1) * 128, :] = gh[:, g * 128 : (g + 1) * 128]


def stage_tenant(own, bias_sm, WR, C2, HT, PL, G, send):
    mask = iota((64, 128), 0) // 4 == own
    lift2 = dot(WR[...], HT[...])
    ridx = iota((8, 128), 0)
    shifts = []
    for b in range(8):
        a = jnp.zeros((8, 128), f32)
        for r in range(8):
            a = jnp.where(ridx == r, bias_sm[r % 4, (b * 8 + r) // 4], a)
        shifts.append(a)
    lift = lift2[0:64] - lift2[64:128] + jnp.concatenate(shifts, axis=0)
    lift = jnp.where(mask, lift, 0.0).astype(bf16)
    r = iota((128, 64), 0)
    c = iota((128, 64), 1)
    hit = c == (r // 8) * 4 + r % 4
    first = (r // 4) % 2 == 0
    li = dot(jnp.where(hit & first, 1.0, 0.0).astype(bf16), lift).astype(bf16)
    pi = dot(jnp.where(hit, jnp.where(first, -1.0, 1.0), 0.0).astype(bf16), PL[...]).astype(bf16)
    for m in range(4):
        part = dot(li, C2[:, m * 1024 : (m + 1) * 1024])
        part = part + dot_nt(pi, HT[m * 1024 : (m + 1) * 1024, :])
        part = part.astype(bf16)
        for g in range(8):
            G[g % 2, m * 4 + g // 2] = part[:, g * 128 : (g + 1) * 128]
        send(m)


def stage_bwd(m, KV, Q, P, GH, scale, DQ, SB, OWN):
    kt = KV[m, 0].T
    gh = GH[m]
    dp = dot_nt(KV[m, 1], gh)
    wl = P[m]
    w = wl.astype(f32)
    wd = w * dp
    delta = jnp.sum(wd, axis=0, keepdims=True)
    ds = (wd - w * delta).astype(bf16)
    dk = dot(ds, Q[m]) * scale
    dv = dot(wl, gh)
    for s in (1, 2):
        rows = slice(HALO - 128 * s, HALO - 128 * s + 128)
        SB[m, s - 1, 0] = dk[rows].astype(bf16)
        SB[m, s - 1, 1] = dv[rows].astype(bf16)
    OWN[m, 0] = dk[HALO:]
    OWN[m, 1] = dv[HALO:]
    dqt = dot(kt, ds) * scale
    for g in range(8):
        DQ[m * 8 + g] = dqt[:, g * 128 : (g + 1) * 128].T.astype(bf16)


REPS, CTXS, CHIPS = 16, 32, 16
HALO = 256
VMEM_LIMIT = 60 << 20


def kernel(
    q_hbm, c_hbm, k_hbm, v_hbm, w_hbm, r_hbm, starts_hbm, owners_hbm, bias_sm,
    dq_hbm, dk_hbm, dv_hbm, gr_hbm, gp_hbm,
    q_in, c_in, k_in, v_in, w_in, r_in, starts_in, owners_in, in_sem,
    KV, Q, C2, WR, MB, P, HT, GH, PL,
    dq_out, dk_out, dv_out, grad_out, out_sem, DQ,
    halo_send, halo_recv,
    SB, RB, OWN, back_send, back_recv,
    G, R1, one_send, one_recv,
    S2, R2, two_send, two_recv,
    S3, R3, three_send, three_recv,
):
    rep = lax.axis_index("rep")
    ctx = lax.axis_index("ctx")
    chip = ctx // 2
    core = ctx % 2
    mate = ctx + 1 - 2 * core
    scale = 128 ** -0.5

    def there(x):
        return (rep, x)

    row_first = ctx * 128
    lanes = pl.ds(pl.multiple_of(row_first, 128), 128)
    loads = []
    for i, (src, dst) in enumerate((
        (k_hbm, k_in), (v_hbm, v_in),
        (starts_hbm.at[:, lanes], starts_in), (owners_hbm.at[:, lanes], owners_in),
        (q_hbm, q_in), (c_hbm, c_in), (w_hbm, w_in), (r_hbm, r_in),
    )):
        cp = pltpu.make_async_copy(src, dst, in_sem.at[i])
        cp.start()
        loads.append(cp)

    barrier = pltpu.get_barrier_semaphore()
    for d in (1, CTXS - 1):
        pl.semaphore_signal(barrier, inc=1, device_id=there((ctx + d) % CTXS), device_id_type=MESH)
    for d in range(1, CHIPS):
        pl.semaphore_signal(
            barrier, inc=1, device_id=there((ctx + 2 * d) % CTXS), device_id_type=MESH
        )
    for d in range(1, REPS):
        pl.semaphore_signal(
            barrier, inc=1, device_id=((rep + d) % REPS, ctx), device_id_type=MESH
        )

    loads[0].wait()
    loads[1].wait()
    kk = jnp.swapaxes(k_in[...].astype(f32), 0, 1).astype(bf16)
    vv = jnp.swapaxes(v_in[...].astype(f32), 0, 1).astype(bf16)
    for m in range(4):
        KV[m, 0, HALO:] = kk[m]
        KV[m, 1, HALO:] = vv[m]
    for cp in loads[2:]:
        cp.wait()
    stage_prep(q_in, c_in, w_in, r_in, Q, C2, WR)
    own = owners_in[...]
    stage_mask(starts_in[...], row_first, MB)

    pl.semaphore_wait(barrier, 2 + (CHIPS - 1) + (REPS - 1))

    def halo_copy(m, s):
        return pltpu.make_async_remote_copy(
            src_ref=KV.at[m, :, pl.ds(HALO, 128)],
            dst_ref=KV.at[m, :, pl.ds(HALO - 128 * s, 128)],
            send_sem=halo_send.at[m, s - 1],
            recv_sem=halo_recv.at[m, s - 1],
            device_id=there((ctx + s) % CTXS),
            device_id_type=MESH,
        )

    for m in range(4):
        for s in (1, 2):
            halo_copy(m, s).start()

    stage_pull(own, WR, C2, GH, PL)

    def fwd(m, carry):
        for s in (1, 2):
            halo_copy(m, s).wait_recv()
        stage_fwd(m, KV, Q, MB, P, HT, scale)
        return carry

    lax.fori_loop(0, 4, fwd, 0)

    def one_copy(m):
        return pltpu.make_async_remote_copy(
            src_ref=G.at[1 - core, pl.ds(4 * m, 4)],
            dst_ref=R1.at[pl.ds(4 * m, 4)],
            send_sem=one_send.at[m],
            recv_sem=one_recv.at[m],
            device_id=there(mate),
            device_id_type=MESH,
        )

    def two_copy(d):
        return pltpu.make_async_remote_copy(
            src_ref=S2.at[(chip + d) % CHIPS],
            dst_ref=R2.at[d],
            send_sem=two_send.at[d],
            recv_sem=two_recv.at[d],
            device_id=there((ctx + 2 * d) % CTXS),
            device_id_type=MESH,
        )

    def three_copy(d):
        return pltpu.make_async_remote_copy(
            src_ref=S3.at[(rep + d) % REPS],
            dst_ref=R3.at[d],
            send_sem=three_send.at[d],
            recv_sem=three_recv.at[d],
            device_id=((rep + d) % REPS, ctx),
            device_id_type=MESH,
        )

    def back_copy(m, s):
        return pltpu.make_async_remote_copy(
            src_ref=SB.at[m, s - 1],
            dst_ref=RB.at[m, s - 1],
            send_sem=back_send.at[m, s - 1],
            recv_sem=back_recv.at[m, s - 1],
            device_id=there((ctx + CTXS - s) % CTXS),
            device_id_type=MESH,
        )

    stage_tenant(own, bias_sm, WR, C2, HT, PL, G, lambda m: one_copy(m).start())

    def bwd(m, carry):
        stage_bwd(m, KV, Q, P, GH, scale, DQ, SB, OWN)
        for s in (1, 2):
            back_copy(m, s).start()

        @pl.when(m == 0)
        def _():
            for i in range(4):
                one_copy(i).wait_recv()
            S2[...] = (G[core].astype(f32) + R1[...].astype(f32)).astype(bf16)
            for d in range(1, CHIPS):
                two_copy(d).start()

        @pl.when(m == 2)
        def _():
            total = S2[chip].astype(f32)
            for d in range(1, CHIPS):
                two_copy(d).wait_recv()
                total = total + R2[d].astype(f32)
            S3[...] = total.reshape(REPS, 8, 128)
            for d in range(1, REPS):
                three_copy(d).start()

        return carry

    lax.fori_loop(0, 4, bwd, 0)

    stores = []
    for m in range(4):
        heads = slice(8 * m, 8 * m + 8)
        dq_out[:, heads, :] = jnp.swapaxes(DQ[heads], 0, 1)
        cp = pltpu.make_async_copy(dq_out.at[:, heads], dq_hbm.at[:, heads], out_sem.at[m])
        cp.start()
        stores.append(cp)

    mine = S3[rep]
    for d in range(1, REPS):
        three_copy(d).wait_recv()
        mine = mine + R3[d]
    grad_out[0] = mine[0:4]
    grad_out[1] = mine[4:8]
    for i, dst in enumerate((gr_hbm, gp_hbm)):
        cp = pltpu.make_async_copy(grad_out.at[i], dst, out_sem.at[4 + i])
        cp.start()
        stores.append(cp)

    for m in range(4):
        for s in (1, 2):
            back_copy(m, s).wait_recv()
    total = OWN[...] + RB[:, 0].astype(f32) + RB[:, 1].astype(f32)
    dk_out[...] = jnp.swapaxes(total[:, 0], 0, 1).astype(bf16)
    dv_out[...] = jnp.swapaxes(total[:, 1], 0, 1).astype(bf16)
    for i, (src, dst) in enumerate(((dk_out, dk_hbm), (dv_out, dv_hbm))):
        cp = pltpu.make_async_copy(src, dst, out_sem.at[6 + i])
        cp.start()
        stores.append(cp)

    for m in range(4):
        one_copy(m).wait_send()
        for s in (1, 2):
            halo_copy(m, s).wait_send()
            back_copy(m, s).wait_send()
    for d in range(1, CHIPS):
        two_copy(d).wait_send()
    for d in range(1, REPS):
        three_copy(d).wait_send()
    for cp in stores:
        cp.wait()


def finish(*refs):
    srcs, dsts, bufs, sems = refs[:5], refs[5:10], refs[10:15], refs[15]
    moves = [(srcs[i], bufs[i], dsts[i]) for i in range(1, 5)]
    for i in range(4):
        rows = pl.ds(32 * i, 32)
        moves.append((srcs[0].at[rows], bufs[0].at[rows], dsts[0].at[rows]))
    loads, stores = [], []
    for i, (src, buf, dst) in enumerate(moves):
        loads.append(pltpu.make_async_copy(src, buf, sems.at[0, i]))
        stores.append(pltpu.make_async_copy(buf, dst, sems.at[1, i]))
        loads[i].start()
    for load, store in zip(loads, stores):
        load.wait()
        store.start()
    for store in stores:
        store.wait()


def on_device(
    query_rows, key_rows, value_matrix, cotangent, rotation, projection, shift_bias,
    doc_starts, tenant_ids,
):
    smem = pl.BlockSpec(memory_space=pltpu.SMEM)
    hbm = pl.BlockSpec(memory_space=pltpu.HBM)
    dma = pltpu.SemaphoreType.DMA
    rows = (128, 32, 128)
    kv_rows = (128, 4, 128)
    out_shape = (
        jax.ShapeDtypeStruct(rows, bf16),
        jax.ShapeDtypeStruct(kv_rows, bf16),
        jax.ShapeDtypeStruct(kv_rows, bf16),
        jax.ShapeDtypeStruct((4, 128), f32),
        jax.ShapeDtypeStruct((4, 128), f32),
    )
    out = pl.pallas_call(
        kernel,
        out_shape=out_shape,
        in_specs=[hbm] * 8 + [smem],
        out_specs=(hbm,) * 5,
        scratch_shapes=[
            pltpu.VMEM(rows, bf16), pltpu.VMEM(rows, bf16),
            pltpu.VMEM((128, 4, 128), bf16), pltpu.VMEM((128, 4, 128), bf16),
            pltpu.VMEM((64, 32, 128), bf16), pltpu.VMEM((64, 32, 128), bf16),
            pltpu.VMEM((1, 128), jnp.int32), pltpu.VMEM((1, 128), jnp.int32),
            dma((8,)),
            pltpu.VMEM((4, 2, 384, 128), bf16),
            pltpu.VMEM((4, 1024, 128), bf16),
            pltpu.VMEM((128, 4096), bf16),
            pltpu.VMEM((128, 4096), bf16),
            pltpu.VMEM((384, 128), f32),
            pltpu.VMEM((4, 384, 1024), bf16),
            pltpu.VMEM((4096, 128), bf16),
            pltpu.VMEM((4, 1024, 128), bf16),
            pltpu.VMEM((64, 128), bf16),
            pltpu.VMEM(rows, bf16), pltpu.VMEM((128, 4, 128), bf16), pltpu.VMEM((128, 4, 128), bf16),
            pltpu.VMEM((2, 4, 128), f32), dma((8,)),
            pltpu.VMEM((32, 128, 128), bf16),
            dma((4, 2)), dma((4, 2)),
            pltpu.VMEM((4, 2, 2, 128, 128), bf16),
            pltpu.VMEM((4, 2, 2, 128, 128), bf16),
            pltpu.VMEM((4, 2, 128, 128), f32),
            dma((4, 2)), dma((4, 2)),
            pltpu.VMEM((2, CHIPS, 128, 128), bf16),
            pltpu.VMEM((CHIPS, 128, 128), bf16),
            dma((4,)), dma((4,)),
            pltpu.VMEM((CHIPS, 128, 128), bf16),
            pltpu.VMEM((CHIPS, 128, 128), bf16),
            dma((CHIPS,)), dma((CHIPS,)),
            pltpu.VMEM((REPS, 8, 128), f32),
            pltpu.VMEM((REPS, 8, 128), f32),
            dma((REPS,)), dma((REPS,)),
        ],
        compiler_params=pltpu.CompilerParams(
            collective_id=0, has_side_effects=True, vmem_limit_bytes=VMEM_LIMIT
        ),
        name="steered_attention_backward",
    )(
        query_rows[0], cotangent[0], key_rows[0], value_matrix[0],
        projection.reshape(64, 32, 128), rotation.reshape(64, 32, 128),
        doc_starts, tenant_ids, shift_bias.T,
    )
    dq, dk, dv, gr, gp = pl.pallas_call(
        finish,
        out_shape=out_shape,
        in_specs=[hbm] * 5,
        out_specs=(hbm,) * 5,
        scratch_shapes=[pltpu.VMEM(s.shape, s.dtype) for s in out_shape] + [dma((2, 8))],
        compiler_params=pltpu.CompilerParams(vmem_limit_bytes=VMEM_LIMIT),
        name="finish",
    )(*out)
    return dq[None], dk[None], dv[None], gr.reshape(1, 4, 1, 128), gp.reshape(1, 4, 1, 128)


def solution(mesh):
    row = P_("rep", "ctx", None, None)
    in_specs = (row, row, row, row, P_(), P_(), P_(), P_("rep", None), P_("rep", None))
    grads = P_("rep", None, "ctx", None)
    return jax.shard_map(
        on_device, mesh=mesh, in_specs=in_specs, out_specs=(row, row, row, grads, grads),
        check_vma=False,
    )
```

```python
import jax
import jax.numpy as jnp
from jax import lax
from jax.experimental import pallas as pl
from jax.experimental.pallas import tpu as pltpu
from jax.sharding import PartitionSpec as P_

f32, bf16 = jnp.float32, jnp.bfloat16
MESH = pl.DeviceIdType.MESH
LOG2E = 1.4426950408889634


def dot(a, b):
    return jnp.dot(a, b, preferred_element_type=f32)


def dot_nt(a, b):
    return lax.dot_general(a, b, (((1,), (1,)), ((), ())), preferred_element_type=f32)


def iota(shape, d):
    return lax.broadcasted_iota(jnp.int32, shape, d)


def stage_prep(q_ref, c_ref, w_ref, r_ref, Q, C2, WR):
    for m in range(4):
        Q[m] = jnp.swapaxes(q_ref[:, 8 * m : 8 * m + 8, :], 0, 1).reshape(1024, 128)
    C2[...] = c_ref[...].reshape(128, 4096)
    WR[0:64] = w_ref[...].reshape(64, 4096)
    WR[64:128] = r_ref[...].reshape(64, 4096)


def stage_mask(starts, row_first, MB):
    key_place = row_first - 256 + iota((384, 128), 0)
    query_place = row_first + iota((384, 128), 1)
    allowed = (key_place >= starts) & (key_place <= query_place)
    MB[...] = jnp.where(allowed, 0.0, -1e30).astype(f32)


def stage_fwd(m, KV, Q, MB, P, HT, scale):
    vt = KV[m, 1].T
    st = dot_nt(KV[m, 0], Q[m])
    s = st * (scale * LOG2E) + jnp.concatenate([MB[...]] * 8, axis=1)
    e = jnp.exp2(s - jnp.max(s, axis=0, keepdims=True))
    wl = (e * (1.0 / jnp.sum(e, axis=0, keepdims=True))).astype(bf16)
    P[m] = wl
    ht = dot(vt, wl).astype(bf16)
    for g in range(8):
        HT[pl.ds(m * 1024 + g * 128, 128), :] = ht[:, g * 128 : (g + 1) * 128]


def stage_pull(own, WR, C2, GH, PP):
    mask = iota((64, 128), 0) // 4 == own
    pull = jnp.where(mask, dot_nt(WR[64:128], C2[...]), 0.0)
    swap = iota((64, 64), 1) == (iota((64, 64), 0) ^ 4)
    PP[...] = dot(jnp.where(swap, 1.0, 0.0).astype(bf16), pull.astype(bf16)).astype(bf16)
    pt = jnp.concatenate([pull, -pull], axis=0).T.astype(bf16)
    for m in range(4):
        cols = slice(m * 1024, (m + 1) * 1024)
        gh = (dot(pt, WR[:, cols]) + C2[:, cols].astype(f32)).astype(bf16)
        for g in range(8):
            GH[m, g * 128 : (g + 1) * 128, :] = gh[:, g * 128 : (g + 1) * 128]


def split_heads(part, m, G):
    part = part.astype(bf16)
    for g in range(8):
        G[g % 2, m * 4 + g // 2] = part[:, g * 128 : (g + 1) * 128]


def stage_projection(m, WR, HT, PP, LIFT, G):
    hidden = HT[pl.ds(m * 1024, 1024), :]
    LIFT[...] += dot(WR[:, pl.ds(pl.multiple_of(m * 1024, 1024), 1024)], hidden)
    split_heads(dot_nt(PP[...], hidden), m, G)


def stage_rotation(own, bias_sm, C2, LIFT, G, send):
    mask = iota((64, 128), 0) // 4 == own
    ridx = iota((8, 128), 0)
    shifts = []
    for b in range(8):
        a = jnp.zeros((8, 128), f32)
        for r in range(8):
            a = jnp.where(ridx == r, bias_sm[r % 4, (b * 8 + r) // 4], a)
        shifts.append(a)
    lift = LIFT[0:64] - LIFT[64:128] + jnp.concatenate(shifts, axis=0)
    lift = jnp.where(mask, lift, 0.0).astype(bf16)
    for m in range(4):
        split_heads(dot(lift, C2[:, m * 1024 : (m + 1) * 1024]), m, G)
        send(m)


def stage_bwd(m, KV, Q, P, GH, scale, DQ, SB, OWN):
    kt = KV[m, 0].T
    gh = GH[m]
    dp = dot_nt(KV[m, 1], gh)
    wl = P[m]
    w = wl.astype(f32)
    wd = w * dp
    delta = jnp.sum(wd, axis=0, keepdims=True)
    ds = (wd - w * delta).astype(bf16)
    dk = dot(ds, Q[m]) * scale
    dv = dot(wl, gh)
    for s in (1, 2):
        rows = slice(HALO - 128 * s, HALO - 128 * s + 128)
        SB[m, s - 1, 0] = dk[rows].astype(bf16)
        SB[m, s - 1, 1] = dv[rows].astype(bf16)
    OWN[m, 0] = dk[HALO:]
    OWN[m, 1] = dv[HALO:]
    dqt = dot(kt, ds) * scale
    for g in range(8):
        DQ[m * 8 + g] = dqt[:, g * 128 : (g + 1) * 128].T.astype(bf16)


REPS, CTXS, CHIPS = 16, 32, 16
HALO = 256
VMEM_LIMIT = 60 << 20


def kernel(
    q_hbm, c_hbm, k_hbm, v_hbm, w_hbm, r_hbm, starts_hbm, owners_hbm, bias_sm,
    dq_hbm, dk_hbm, dv_hbm, gr_hbm, gp_hbm,
    q_in, c_in, k_in, v_in, w_in, r_in, starts_in, owners_in, in_sem,
    KV, Q, C2, WR, MB, P, HT, GH, PP, LIFT,
    dq_out, dk_out, dv_out, grad_out, out_sem, DQ,
    halo_send, halo_recv, met,
    SB, RB, OWN, back_send, back_recv,
    G, R1, one_send, one_recv,
    S2, R2, two_send, two_recv,
    S3, R3, three_send, three_recv,
):
    rep = lax.axis_index("rep")
    ctx = lax.axis_index("ctx")
    chip = ctx // 2
    core = ctx % 2
    mate = ctx + 1 - 2 * core
    scale = 128 ** -0.5

    def there(x):
        return (rep, x)

    row_first = ctx * 128
    lanes = pl.ds(pl.multiple_of(row_first, 128), 128)
    loads = []
    for i, (src, dst) in enumerate((
        (k_hbm, k_in), (v_hbm, v_in),
        (starts_hbm.at[:, lanes], starts_in), (owners_hbm.at[:, lanes], owners_in),
        (q_hbm, q_in), (c_hbm, c_in), (w_hbm, w_in), (r_hbm, r_in),
    )):
        cp = pltpu.make_async_copy(src, dst, in_sem.at[i])
        cp.start()
        loads.append(cp)

    barrier = pltpu.get_barrier_semaphore()
    for d in [1, CTXS - 1] + list(range(2, CTXS, 2)):
        pl.semaphore_signal(barrier, inc=1, device_id=there((ctx + d) % CTXS), device_id_type=MESH)

    def along_z(d):
        return ((rep + d) % REPS, ctx)

    def greet_z(sem, d):
        for x in (d, REPS - d):
            pl.semaphore_signal(sem, inc=1, device_id=along_z(x), device_id_type=MESH)

    greet_z(barrier, 1)

    loads[0].wait()
    loads[1].wait()
    kk = jnp.swapaxes(k_in[...].astype(f32), 0, 1).astype(bf16)
    vv = jnp.swapaxes(v_in[...].astype(f32), 0, 1).astype(bf16)
    for m in range(4):
        KV[m, 0, HALO:] = kk[m]
        KV[m, 1, HALO:] = vv[m]
    pl.semaphore_wait(barrier, 2 + (CHIPS - 1) + 2)
    greet_z(met.at[0], 1)

    def far_copy(m):
        return pltpu.make_async_remote_copy(
            src_ref=KV.at[m, :, pl.ds(HALO, 128)],
            dst_ref=KV.at[m, :, pl.ds(0, 128)],
            send_sem=halo_send.at[m, 1],
            recv_sem=halo_recv.at[m, 1],
            device_id=there((ctx + 2) % CTXS),
            device_id_type=MESH,
        )

    def near_copy(m):
        return pltpu.make_async_remote_copy(
            src_ref=KV.at[m, :, pl.ds(pl.multiple_of(HALO * (1 - core), 128), 128)],
            dst_ref=KV.at[m, :, pl.ds(128, 128)],
            send_sem=halo_send.at[m, 0],
            recv_sem=halo_recv.at[m, 0],
            device_id=there(mate),
            device_id_type=MESH,
        )

    for m in range(4):
        far_copy(m).start()

    @pl.when(core == 0)
    def _():
        for m in range(4):
            near_copy(m).start()

    for cp in loads[2:]:
        cp.wait()
    stage_prep(q_in, c_in, w_in, r_in, Q, C2, WR)
    own = owners_in[...]
    stage_mask(starts_in[...], row_first, MB)
    stage_pull(own, WR, C2, GH, PP)
    LIFT[...] = jnp.zeros_like(LIFT)
    pl.semaphore_wait(met.at[0], 2)
    greet_z(met.at[1], 2)

    def one_copy(p, m):
        return pltpu.make_async_remote_copy(
            src_ref=G.at[p, 1 - core, pl.ds(4 * m, 4)],
            dst_ref=R1.at[p, pl.ds(4 * m, 4)],
            send_sem=one_send.at[p, m],
            recv_sem=one_recv.at[p, m],
            device_id=there(mate),
            device_id_type=MESH,
        )

    def two_copy(d):
        return pltpu.make_async_remote_copy(
            src_ref=S2.at[(chip + d) % CHIPS],
            dst_ref=R2.at[d],
            send_sem=two_send.at[d],
            recv_sem=two_recv.at[d],
            device_id=there((ctx + 2 * d) % CTXS),
            device_id_type=MESH,
        )

    def pair_sum(p, m):
        one_copy(p, m).wait_recv()
        part = pl.ds(4 * m, 4)
        S2[part, p] = (G[p, core, part].astype(f32) + R1[p, part].astype(f32)).astype(bf16)

    def chip_sum():
        total = S2[chip].astype(f32)
        for d in range(1, CHIPS):
            two_copy(d).wait_recv()
            total = total + R2[d].astype(f32)
        return total[0], total[1]

    def three_copy(d):
        return pltpu.make_async_remote_copy(
            src_ref=S3.at[(rep + d) % REPS],
            dst_ref=R3.at[d],
            send_sem=three_send.at[d],
            recv_sem=three_recv.at[d],
            device_id=along_z(d),
            device_id_type=MESH,
        )

    def fwd(m, carry):
        far_copy(m).wait_recv()

        @pl.when(core == 1)
        def _():
            near_copy(m).start()

        near_copy(m).wait_recv()
        stage_fwd(m, KV, Q, MB, P, HT, scale)
        stage_projection(m, WR, HT, PP, LIFT, G.at[1])
        one_copy(1, m).start()

        return carry

    lax.fori_loop(0, 4, fwd, 0)
    pl.semaphore_wait(met.at[1], 2)
    greet_z(met.at[2], 4)

    def back_copy(m, s):
        return pltpu.make_async_remote_copy(
            src_ref=SB.at[m, s - 1],
            dst_ref=RB.at[m, s - 1],
            send_sem=back_send.at[m, s - 1],
            recv_sem=back_recv.at[m, s - 1],
            device_id=there((ctx + CTXS - s) % CTXS),
            device_id_type=MESH,
        )

    stage_rotation(own, bias_sm, C2, LIFT, G.at[0], lambda m: one_copy(0, m).start())
    for m in range(4):
        pair_sum(1, m)

    def bwd(m, carry):
        stage_bwd(m, KV, Q, P, GH, scale, DQ, SB, OWN)

        @pl.when(m == 0)
        def _():
            for i in range(4):
                pair_sum(0, i)
            for d in range(1, CHIPS):
                two_copy(d).start()

        for s in (1, 2):
            back_copy(m, s).start()
        return carry

    lax.fori_loop(0, 4, bwd, 0)
    rot, proj = chip_sum()
    upper = iota((8, 128), 0) < 4
    for t in range(0, REPS, 2):
        a, c = rot[4 * t : 4 * t + 8], proj[4 * t : 4 * t + 8]
        S3[t] = jnp.where(upper, a, c)
        S3[t + 1] = jnp.where(upper, c, a)
    pl.semaphore_wait(met.at[2], 2)
    for d in range(1, REPS):
        three_copy(d).start()

    stores = []
    for m in range(4):
        heads = slice(8 * m, 8 * m + 8)
        dq_out[:, heads, :] = jnp.swapaxes(DQ[heads], 0, 1)
        cp = pltpu.make_async_copy(dq_out.at[:, heads], dq_hbm.at[:, heads], out_sem.at[m])
        cp.start()
        stores.append(cp)

    for m in range(4):
        for s in (1, 2):
            back_copy(m, s).wait_recv()
    total = OWN[...] + RB[:, 0].astype(f32) + RB[:, 1].astype(f32)
    dk_out[...] = jnp.swapaxes(total[:, 0], 0, 1).astype(bf16)
    dv_out[...] = jnp.swapaxes(total[:, 1], 0, 1).astype(bf16)
    for i, (src, dst) in enumerate(((dk_out, dk_hbm), (dv_out, dv_hbm))):
        cp = pltpu.make_async_copy(src, dst, out_sem.at[6 + i])
        cp.start()
        stores.append(cp)

    mine = S3[rep]
    for d in range(1, REPS):
        three_copy(d).wait_recv()
        mine = mine + R3[d]
    odd = rep % 2 == 1
    low, high = mine[0:4], mine[4:8]
    proj = jnp.where(odd, low, high)
    grad_out[0] = jnp.where(odd, high, low) - proj
    grad_out[1] = proj
    for i, dst in enumerate((gr_hbm, gp_hbm)):
        cp = pltpu.make_async_copy(grad_out.at[i], dst, out_sem.at[4 + i])
        cp.start()
        stores.append(cp)

    for m in range(4):
        one_copy(0, m).wait_send()
        one_copy(1, m).wait_send()
        far_copy(m).wait_send()
        near_copy(m).wait_send()
        for s in (1, 2):
            back_copy(m, s).wait_send()
    for d in range(1, CHIPS):
        two_copy(d).wait_send()
    for d in range(1, REPS):
        three_copy(d).wait_send()
    for cp in stores:
        cp.wait()


def finish(*refs):
    srcs, dsts, bufs, sems = refs[:5], refs[5:10], refs[10:15], refs[15]
    moves = [(srcs[i], bufs[i], dsts[i]) for i in range(1, 5)]
    for i in range(4):
        rows = pl.ds(32 * i, 32)
        moves.append((srcs[0].at[rows], bufs[0].at[rows], dsts[0].at[rows]))
    loads, stores = [], []
    for i, (src, buf, dst) in enumerate(moves):
        loads.append(pltpu.make_async_copy(src, buf, sems.at[0, i]))
        stores.append(pltpu.make_async_copy(buf, dst, sems.at[1, i]))
        loads[i].start()
    for load, store in zip(loads, stores):
        load.wait()
        store.start()
    for store in stores:
        store.wait()


def on_device(
    query_rows, key_rows, value_matrix, cotangent, rotation, projection, shift_bias,
    doc_starts, tenant_ids,
):
    smem = pl.BlockSpec(memory_space=pltpu.SMEM)
    hbm = pl.BlockSpec(memory_space=pltpu.HBM)
    dma = pltpu.SemaphoreType.DMA
    rows = (128, 32, 128)
    kv_rows = (128, 4, 128)
    out_shape = (
        jax.ShapeDtypeStruct(rows, bf16),
        jax.ShapeDtypeStruct(kv_rows, bf16),
        jax.ShapeDtypeStruct(kv_rows, bf16),
        jax.ShapeDtypeStruct((4, 128), f32),
        jax.ShapeDtypeStruct((4, 128), f32),
    )
    out = pl.pallas_call(
        kernel,
        out_shape=out_shape,
        in_specs=[hbm] * 8 + [smem],
        out_specs=(hbm,) * 5,
        scratch_shapes=[
            pltpu.VMEM(rows, bf16), pltpu.VMEM(rows, bf16),
            pltpu.VMEM((128, 4, 128), bf16), pltpu.VMEM((128, 4, 128), bf16),
            pltpu.VMEM((64, 32, 128), bf16), pltpu.VMEM((64, 32, 128), bf16),
            pltpu.VMEM((1, 128), jnp.int32), pltpu.VMEM((1, 128), jnp.int32),
            dma((8,)),
            pltpu.VMEM((4, 2, 384, 128), bf16),
            pltpu.VMEM((4, 1024, 128), bf16),
            pltpu.VMEM((128, 4096), bf16),
            pltpu.VMEM((128, 4096), bf16),
            pltpu.VMEM((384, 128), f32),
            pltpu.VMEM((4, 384, 1024), bf16),
            pltpu.VMEM((4096, 128), bf16),
            pltpu.VMEM((4, 1024, 128), bf16),
            pltpu.VMEM((64, 128), bf16),
            pltpu.VMEM((128, 128), f32),
            pltpu.VMEM(rows, bf16), pltpu.VMEM((128, 4, 128), bf16), pltpu.VMEM((128, 4, 128), bf16),
            pltpu.VMEM((2, 4, 128), f32), dma((8,)),
            pltpu.VMEM((32, 128, 128), bf16),
            dma((4, 2)), dma((4, 2)), pltpu.SemaphoreType.REGULAR((3,)),
            pltpu.VMEM((4, 2, 2, 128, 128), bf16),
            pltpu.VMEM((4, 2, 2, 128, 128), bf16),
            pltpu.VMEM((4, 2, 128, 128), f32),
            dma((4, 2)), dma((4, 2)),
            pltpu.VMEM((2, 2, CHIPS, 64, 128), bf16),
            pltpu.VMEM((2, CHIPS, 64, 128), bf16),
            dma((2, 4)), dma((2, 4)),
            pltpu.VMEM((CHIPS, 2, 64, 128), bf16),
            pltpu.VMEM((CHIPS, 2, 64, 128), bf16),
            dma((CHIPS,)), dma((CHIPS,)),
            pltpu.VMEM((REPS, 8, 128), f32),
            pltpu.VMEM((REPS, 8, 128), f32),
            dma((REPS,)), dma((REPS,)),
        ],
        compiler_params=pltpu.CompilerParams(
            collective_id=0, has_side_effects=True, vmem_limit_bytes=VMEM_LIMIT
        ),
        name="steered_attention_backward",
    )(
        query_rows[0], cotangent[0], key_rows[0], value_matrix[0],
        projection.reshape(64, 32, 128), rotation.reshape(64, 32, 128),
        doc_starts, tenant_ids, shift_bias.T,
    )
    dq, dk, dv, gr, gp = pl.pallas_call(
        finish,
        out_shape=out_shape,
        in_specs=[hbm] * 5,
        out_specs=(hbm,) * 5,
        scratch_shapes=[pltpu.VMEM(s.shape, s.dtype) for s in out_shape] + [dma((2, 8))],
        compiler_params=pltpu.CompilerParams(vmem_limit_bytes=VMEM_LIMIT),
        name="finish",
    )(*out)
    return dq[None], dk[None], dv[None], gr.reshape(1, 4, 1, 128), gp.reshape(1, 4, 1, 128)


def solution(mesh):
    row = P_("rep", "ctx", None, None)
    in_specs = (row, row, row, row, P_(), P_(), P_(), P_("rep", None), P_("rep", None))
    grads = P_("rep", None, "ctx", None)
    return jax.shard_map(
        on_device, mesh=mesh, in_specs=in_specs, out_specs=(row, row, row, grads, grads),
        check_vma=False,
    )
```

```python
import jax
import jax.numpy as jnp
from jax import lax
from jax.experimental import pallas as pl
from jax.experimental.pallas import tpu as pltpu
from jax.sharding import PartitionSpec as P_

f32, bf16 = jnp.float32, jnp.bfloat16
MESH = pl.DeviceIdType.MESH
LOG2E = 1.4426950408889634


def dot(a, b):
    return jnp.dot(a, b, preferred_element_type=f32)


def dot_nt(a, b):
    return lax.dot_general(a, b, (((1,), (1,)), ((), ())), preferred_element_type=f32)


def iota(shape, d):
    return lax.broadcasted_iota(jnp.int32, shape, d)


def stage_prep(q_ref, c_ref, w_ref, r_ref, Q, C2, WR):
    for m in range(4):
        Q[m] = jnp.swapaxes(q_ref[:, 8 * m : 8 * m + 8, :], 0, 1).reshape(1024, 128)
    C2[...] = c_ref[...].reshape(128, 4096)
    WR[0:64] = w_ref[...].reshape(64, 4096)
    WR[64:128] = r_ref[...].reshape(64, 4096)


def stage_mask(starts, row_first, MB):
    key_place = row_first - 256 + iota((384, 128), 0)
    query_place = row_first + iota((384, 128), 1)
    allowed = (key_place >= starts) & (key_place <= query_place)
    MB[...] = jnp.where(allowed, 0.0, -1e30).astype(f32)


def stage_fwd(m, KV, Q, MB, P, HT, scale):
    vt = KV[m, 1].T
    st = dot_nt(KV[m, 0], Q[m])
    s = st * (scale * LOG2E) + jnp.concatenate([MB[...]] * 8, axis=1)
    e = jnp.exp2(s - jnp.max(s, axis=0, keepdims=True))
    wl = (e * (1.0 / jnp.sum(e, axis=0, keepdims=True))).astype(bf16)
    P[m] = wl
    ht = dot(vt, wl).astype(bf16)
    for g in range(8):
        HT[pl.ds(m * 1024 + g * 128, 128), :] = ht[:, g * 128 : (g + 1) * 128]


def stage_pull(own, WR, C2, PP, PT):
    mask = iota((64, 128), 0) // 4 == own
    pull = jnp.where(mask, dot_nt(WR[64:128], C2[...]), 0.0)
    swap = iota((64, 64), 1) == (iota((64, 64), 0) ^ 4)
    PP[...] = dot(jnp.where(swap, 1.0, 0.0).astype(bf16), pull.astype(bf16)).astype(bf16)
    PT[...] = jnp.concatenate([pull, -pull], axis=0).T.astype(bf16)


def stage_grad_hidden(WR, C2, PT, GH):
    pt = PT[...]
    for m in range(4):
        cols = slice(m * 1024, (m + 1) * 1024)
        gh = (dot(pt, WR[:, cols]) + C2[:, cols].astype(f32)).astype(bf16)
        for g in range(8):
            GH[m, g * 128 : (g + 1) * 128, :] = gh[:, g * 128 : (g + 1) * 128]


def split_heads(part, m, G):
    part = part.astype(bf16)
    for g in range(8):
        G[g % 2, m * 4 + g // 2] = part[:, g * 128 : (g + 1) * 128]


def stage_projection(m, WR, HT, PP, LIFT, G):
    hidden = HT[pl.ds(m * 1024, 1024), :]
    LIFT[...] += dot(WR[:, pl.ds(pl.multiple_of(m * 1024, 1024), 1024)], hidden)
    split_heads(dot_nt(PP[...], hidden), m, G)


def stage_rotation(own, bias_sm, C2, LIFT, G, send):
    mask = iota((64, 128), 0) // 4 == own
    ridx = iota((8, 128), 0)
    shifts = []
    for b in range(8):
        a = jnp.zeros((8, 128), f32)
        for r in range(8):
            a = jnp.where(ridx == r, bias_sm[r % 4, (b * 8 + r) // 4], a)
        shifts.append(a)
    lift = LIFT[0:64] - LIFT[64:128] + jnp.concatenate(shifts, axis=0)
    lift = jnp.where(mask, lift, 0.0).astype(bf16)
    for m in range(4):
        split_heads(dot(lift, C2[:, m * 1024 : (m + 1) * 1024]), m, G)
        send(m)


def stage_bwd(m, KV, Q, P, GH, scale, DQ, SB, OWN):
    kt = KV[m, 0].T
    gh = GH[m]
    dp = dot_nt(KV[m, 1], gh)
    wl = P[m]
    w = wl.astype(f32)
    wd = w * dp
    delta = jnp.sum(wd, axis=0, keepdims=True)
    ds = (wd - w * delta).astype(bf16)
    dk = dot(ds, Q[m]) * scale
    dv = dot(wl, gh)
    for s in (1, 2):
        rows = slice(HALO - 128 * s, HALO - 128 * s + 128)
        SB[m, s - 1, 0] = dk[rows].astype(bf16)
        SB[m, s - 1, 1] = dv[rows].astype(bf16)
    OWN[m, 0] = dk[HALO:]
    OWN[m, 1] = dv[HALO:]
    dqt = dot(kt, ds) * scale
    for g in range(8):
        DQ[m * 8 + g] = dqt[:, g * 128 : (g + 1) * 128].T.astype(bf16)


REPS, CTXS, CHIPS = 16, 32, 16
HALO = 256
VMEM_LIMIT = 60 << 20


def kernel(
    q_hbm, c_hbm, k_hbm, v_hbm, w_hbm, r_hbm, starts_hbm, owners_hbm, bias_sm,
    dq_hbm, dk_hbm, dv_hbm, gr_hbm, gp_hbm,
    q_in, c_in, k_in, v_in, w_in, r_in, starts_in, owners_in, in_sem,
    KV, Q, C2, WR, MB, P, HT, GH, PP, PT, LIFT,
    dq_out, dk_out, dv_out, grad_out, out_sem, DQ,
    halo_send, halo_recv, met,
    SB, RB, OWN, back_send, back_recv,
    G, R1, one_send, one_recv,
    S2, R2, two_send, two_recv,
    S3, R3, three_send, three_recv,
):
    rep = lax.axis_index("rep")
    ctx = lax.axis_index("ctx")
    chip = ctx // 2
    core = ctx % 2
    mate = ctx + 1 - 2 * core
    scale = 128 ** -0.5

    def there(x):
        return (rep, x)

    row_first = ctx * 128
    lanes = pl.ds(pl.multiple_of(row_first, 128), 128)
    loads = []
    for i, (src, dst) in enumerate((
        (k_hbm, k_in), (v_hbm, v_in),
        (starts_hbm.at[:, lanes], starts_in), (owners_hbm.at[:, lanes], owners_in),
        (q_hbm, q_in), (c_hbm, c_in), (w_hbm, w_in), (r_hbm, r_in),
    )):
        cp = pltpu.make_async_copy(src, dst, in_sem.at[i])
        cp.start()
        loads.append(cp)

    barrier = pltpu.get_barrier_semaphore()
    for d in [1, CTXS - 1] + list(range(2, CTXS, 2)):
        pl.semaphore_signal(barrier, inc=1, device_id=there((ctx + d) % CTXS), device_id_type=MESH)

    def along_z(d):
        return ((rep + d) % REPS, ctx)

    def greet_z(sem, d):
        for x in (d, REPS - d):
            pl.semaphore_signal(sem, inc=1, device_id=along_z(x), device_id_type=MESH)

    greet_z(barrier, 1)

    loads[0].wait()
    loads[1].wait()
    kk = jnp.swapaxes(k_in[...].astype(f32), 0, 1).astype(bf16)
    vv = jnp.swapaxes(v_in[...].astype(f32), 0, 1).astype(bf16)
    for m in range(4):
        KV[m, 0, HALO:] = kk[m]
        KV[m, 1, HALO:] = vv[m]
    pl.semaphore_wait(barrier, 2 + (CHIPS - 1) + 2)
    greet_z(met.at[0], 1)

    def far_copy(m):
        return pltpu.make_async_remote_copy(
            src_ref=KV.at[m, :, pl.ds(HALO, 128)],
            dst_ref=KV.at[m, :, pl.ds(0, 128)],
            send_sem=halo_send.at[m, 1],
            recv_sem=halo_recv.at[m, 1],
            device_id=there((ctx + 2) % CTXS),
            device_id_type=MESH,
        )

    def near_copy(m):
        return pltpu.make_async_remote_copy(
            src_ref=KV.at[m, :, pl.ds(pl.multiple_of(HALO * (1 - core), 128), 128)],
            dst_ref=KV.at[m, :, pl.ds(128, 128)],
            send_sem=halo_send.at[m, 0],
            recv_sem=halo_recv.at[m, 0],
            device_id=there(mate),
            device_id_type=MESH,
        )

    for m in range(4):
        far_copy(m).start()

    @pl.when(core == 0)
    def _():
        for m in range(4):
            near_copy(m).start()

    for cp in loads[2:]:
        cp.wait()
    stage_prep(q_in, c_in, w_in, r_in, Q, C2, WR)
    own = owners_in[...]
    stage_mask(starts_in[...], row_first, MB)
    stage_pull(own, WR, C2, PP, PT)
    LIFT[...] = jnp.zeros_like(LIFT)
    pl.semaphore_wait(met.at[0], 2)
    greet_z(met.at[1], 2)

    def one_copy(p, m):
        return pltpu.make_async_remote_copy(
            src_ref=G.at[p, 1 - core, pl.ds(4 * m, 4)],
            dst_ref=R1.at[p, pl.ds(4 * m, 4)],
            send_sem=one_send.at[p, m],
            recv_sem=one_recv.at[p, m],
            device_id=there(mate),
            device_id_type=MESH,
        )

    def two_copy(p, d):
        return pltpu.make_async_remote_copy(
            src_ref=S2.at[p, (chip + d) % CHIPS],
            dst_ref=R2.at[p, d],
            send_sem=two_send.at[p, d],
            recv_sem=two_recv.at[p, d],
            device_id=there((ctx + 2 * d) % CTXS),
            device_id_type=MESH,
        )

    def pair_sum(p, m):
        one_copy(p, m).wait_recv()
        part = pl.ds(4 * m, 4)
        S2[p, part] = (G[p, core, part].astype(f32) + R1[p, part].astype(f32)).astype(bf16)
        for i in range(4):
            d = (4 * m + i + CHIPS - chip) % CHIPS

            @pl.when(d > 0)
            def _():
                two_copy(p, d).start()

    def chip_sum(p):
        total = S2[p, chip].astype(f32)
        for d in range(1, CHIPS):
            two_copy(p, d).wait_recv()
            total = total + R2[p, d].astype(f32)
        return total

    def spread():
        proj, rot = chip_sum(1), chip_sum(0)
        upper = iota((8, 128), 0) < 4
        for t in range(0, REPS, 2):
            a, c = rot[4 * t : 4 * t + 8], proj[4 * t : 4 * t + 8]
            S3[t] = jnp.where(upper, a, c)
            S3[t + 1] = jnp.where(upper, c, a)
        pl.semaphore_wait(met.at[2], 2)
        for d in range(1, REPS):
            three_copy(d).start()

    def three_copy(d):
        return pltpu.make_async_remote_copy(
            src_ref=S3.at[(rep + d) % REPS],
            dst_ref=R3.at[d],
            send_sem=three_send.at[d],
            recv_sem=three_recv.at[d],
            device_id=along_z(d),
            device_id_type=MESH,
        )

    def fwd(m, carry):
        far_copy(m).wait_recv()

        @pl.when(core == 1)
        def _():
            near_copy(m).start()

        near_copy(m).wait_recv()
        stage_fwd(m, KV, Q, MB, P, HT, scale)
        stage_projection(m, WR, HT, PP, LIFT, G.at[1])
        one_copy(1, m).start()

        return carry

    lax.fori_loop(0, 4, fwd, 0)
    pl.semaphore_wait(met.at[1], 2)
    greet_z(met.at[2], 4)

    def back_copy(m, s):
        return pltpu.make_async_remote_copy(
            src_ref=SB.at[m, s - 1],
            dst_ref=RB.at[m, s - 1],
            send_sem=back_send.at[m, s - 1],
            recv_sem=back_recv.at[m, s - 1],
            device_id=there((ctx + CTXS - s) % CTXS),
            device_id_type=MESH,
        )

    for m in range(3):
        pair_sum(1, m)
    stage_rotation(own, bias_sm, C2, LIFT, G.at[0], lambda m: one_copy(0, m).start())
    pair_sum(1, 3)
    stage_grad_hidden(WR, C2, PT, GH)
    for m in range(4):
        pair_sum(0, m)

    def bwd(m, carry):
        stage_bwd(m, KV, Q, P, GH, scale, DQ, SB, OWN)

        for s in (1, 2):
            back_copy(m, s).start()
        return carry

    lax.fori_loop(0, 4, bwd, 0)
    spread()

    stores = []
    for m in range(4):
        heads = slice(8 * m, 8 * m + 8)
        dq_out[:, heads, :] = jnp.swapaxes(DQ[heads], 0, 1)
        cp = pltpu.make_async_copy(dq_out.at[:, heads], dq_hbm.at[:, heads], out_sem.at[m])
        cp.start()
        stores.append(cp)

    for m in range(4):
        for s in (1, 2):
            back_copy(m, s).wait_recv()
    total = OWN[...] + RB[:, 0].astype(f32) + RB[:, 1].astype(f32)
    dk_out[...] = jnp.swapaxes(total[:, 0], 0, 1).astype(bf16)
    dv_out[...] = jnp.swapaxes(total[:, 1], 0, 1).astype(bf16)
    for i, (src, dst) in enumerate(((dk_out, dk_hbm), (dv_out, dv_hbm))):
        cp = pltpu.make_async_copy(src, dst, out_sem.at[6 + i])
        cp.start()
        stores.append(cp)

    mine = S3[rep]
    for d in range(1, REPS):
        three_copy(d).wait_recv()
        mine = mine + R3[d]
    odd = rep % 2 == 1
    low, high = mine[0:4], mine[4:8]
    proj = jnp.where(odd, low, high)
    grad_out[0] = jnp.where(odd, high, low) - proj
    grad_out[1] = proj
    for i, dst in enumerate((gr_hbm, gp_hbm)):
        cp = pltpu.make_async_copy(grad_out.at[i], dst, out_sem.at[4 + i])
        cp.start()
        stores.append(cp)

    for m in range(4):
        one_copy(0, m).wait_send()
        one_copy(1, m).wait_send()
        far_copy(m).wait_send()
        near_copy(m).wait_send()
        for s in (1, 2):
            back_copy(m, s).wait_send()
    for d in range(1, CHIPS):
        two_copy(0, d).wait_send()
        two_copy(1, d).wait_send()
    for d in range(1, REPS):
        three_copy(d).wait_send()
    for cp in stores:
        cp.wait()


def finish(*refs):
    srcs, dsts, bufs, sems = refs[:5], refs[5:10], refs[10:15], refs[15]
    moves = [(srcs[i], bufs[i], dsts[i]) for i in range(1, 5)]
    for i in range(4):
        rows = pl.ds(32 * i, 32)
        moves.append((srcs[0].at[rows], bufs[0].at[rows], dsts[0].at[rows]))
    loads, stores = [], []
    for i, (src, buf, dst) in enumerate(moves):
        loads.append(pltpu.make_async_copy(src, buf, sems.at[0, i]))
        stores.append(pltpu.make_async_copy(buf, dst, sems.at[1, i]))
        loads[i].start()
    for load, store in zip(loads, stores):
        load.wait()
        store.start()
    for store in stores:
        store.wait()


def on_device(
    query_rows, key_rows, value_matrix, cotangent, rotation, projection, shift_bias,
    doc_starts, tenant_ids,
):
    smem = pl.BlockSpec(memory_space=pltpu.SMEM)
    hbm = pl.BlockSpec(memory_space=pltpu.HBM)
    dma = pltpu.SemaphoreType.DMA
    rows = (128, 32, 128)
    kv_rows = (128, 4, 128)
    out_shape = (
        jax.ShapeDtypeStruct(rows, bf16),
        jax.ShapeDtypeStruct(kv_rows, bf16),
        jax.ShapeDtypeStruct(kv_rows, bf16),
        jax.ShapeDtypeStruct((4, 128), f32),
        jax.ShapeDtypeStruct((4, 128), f32),
    )
    out = pl.pallas_call(
        kernel,
        out_shape=out_shape,
        in_specs=[hbm] * 8 + [smem],
        out_specs=(hbm,) * 5,
        scratch_shapes=[
            pltpu.VMEM(rows, bf16), pltpu.VMEM(rows, bf16),
            pltpu.VMEM((128, 4, 128), bf16), pltpu.VMEM((128, 4, 128), bf16),
            pltpu.VMEM((64, 32, 128), bf16), pltpu.VMEM((64, 32, 128), bf16),
            pltpu.VMEM((1, 128), jnp.int32), pltpu.VMEM((1, 128), jnp.int32),
            dma((8,)),
            pltpu.VMEM((4, 2, 384, 128), bf16),
            pltpu.VMEM((4, 1024, 128), bf16),
            pltpu.VMEM((128, 4096), bf16),
            pltpu.VMEM((128, 4096), bf16),
            pltpu.VMEM((384, 128), f32),
            pltpu.VMEM((4, 384, 1024), bf16),
            pltpu.VMEM((4096, 128), bf16),
            pltpu.VMEM((4, 1024, 128), bf16),
            pltpu.VMEM((64, 128), bf16),
            pltpu.VMEM((128, 128), bf16),
            pltpu.VMEM((128, 128), f32),
            pltpu.VMEM(rows, bf16), pltpu.VMEM((128, 4, 128), bf16), pltpu.VMEM((128, 4, 128), bf16),
            pltpu.VMEM((2, 4, 128), f32), dma((8,)),
            pltpu.VMEM((32, 128, 128), bf16),
            dma((4, 2)), dma((4, 2)), pltpu.SemaphoreType.REGULAR((3,)),
            pltpu.VMEM((4, 2, 2, 128, 128), bf16),
            pltpu.VMEM((4, 2, 2, 128, 128), bf16),
            pltpu.VMEM((4, 2, 128, 128), f32),
            dma((4, 2)), dma((4, 2)),
            pltpu.VMEM((2, 2, CHIPS, 64, 128), bf16),
            pltpu.VMEM((2, CHIPS, 64, 128), bf16),
            dma((2, 4)), dma((2, 4)),
            pltpu.VMEM((2, CHIPS, 64, 128), bf16),
            pltpu.VMEM((2, CHIPS, 64, 128), bf16),
            dma((2, CHIPS)), dma((2, CHIPS)),
            pltpu.VMEM((REPS, 8, 128), f32),
            pltpu.VMEM((REPS, 8, 128), f32),
            dma((REPS,)), dma((REPS,)),
        ],
        compiler_params=pltpu.CompilerParams(
            collective_id=0, has_side_effects=True, vmem_limit_bytes=VMEM_LIMIT
        ),
        name="steered_attention_backward",
    )(
        query_rows[0], cotangent[0], key_rows[0], value_matrix[0],
        projection.reshape(64, 32, 128), rotation.reshape(64, 32, 128),
        doc_starts, tenant_ids, shift_bias.T,
    )
    dq, dk, dv, gr, gp = pl.pallas_call(
        finish,
        out_shape=out_shape,
        in_specs=[hbm] * 5,
        out_specs=(hbm,) * 5,
        scratch_shapes=[pltpu.VMEM(s.shape, s.dtype) for s in out_shape] + [dma((2, 8))],
        compiler_params=pltpu.CompilerParams(vmem_limit_bytes=VMEM_LIMIT),
        name="finish",
    )(*out)
    return dq[None], dk[None], dv[None], gr.reshape(1, 4, 1, 128), gp.reshape(1, 4, 1, 128)


def solution(mesh):
    row = P_("rep", "ctx", None, None)
    in_specs = (row, row, row, row, P_(), P_(), P_(), P_("rep", None), P_("rep", None))
    grads = P_("rep", None, "ctx", None)
    return jax.shard_map(
        on_device, mesh=mesh, in_specs=in_specs, out_specs=(row, row, row, grads, grads),
        check_vma=False,
    )
```

```python
import jax
import jax.numpy as jnp
from jax import lax
from jax.experimental import pallas as pl
from jax.experimental.pallas import tpu as pltpu
from jax.sharding import PartitionSpec as P_

f32, bf16 = jnp.float32, jnp.bfloat16
MESH = pl.DeviceIdType.MESH
LOG2E = 1.4426950408889634


def dot(a, b):
    return jnp.dot(a, b, preferred_element_type=f32)


def dot_nt(a, b):
    return lax.dot_general(a, b, (((1,), (1,)), ((), ())), preferred_element_type=f32)


def iota(shape, d):
    return lax.broadcasted_iota(jnp.int32, shape, d)


def stage_prep(q_ref, c_ref, w_ref, r_ref, Q, C2, WR):
    for m in range(4):
        Q[m] = jnp.swapaxes(q_ref[:, 8 * m : 8 * m + 8, :], 0, 1).reshape(1024, 128)
    C2[...] = c_ref[...].reshape(128, 4096)
    WR[0:64] = w_ref[...].reshape(64, 4096)
    WR[64:128] = r_ref[...].reshape(64, 4096)


def stage_mask(starts, row_first, MB):
    key_place = row_first - 256 + iota((384, 128), 0)
    query_place = row_first + iota((384, 128), 1)
    allowed = (key_place >= starts) & (key_place <= query_place)
    MB[...] = jnp.where(allowed, 0.0, -1e30).astype(f32)


def stage_fwd(m, KV, Q, MB, P, HT, scale):
    vt = KV[m, 1].T
    st = dot_nt(KV[m, 0], Q[m])
    s = st * (scale * LOG2E) + jnp.concatenate([MB[...]] * 8, axis=1)
    e = jnp.exp2(s - jnp.max(s, axis=0, keepdims=True))
    wl = (e * (1.0 / jnp.sum(e, axis=0, keepdims=True))).astype(bf16)
    P[m] = wl
    ht = dot(vt, wl).astype(bf16)
    for g in range(8):
        HT[pl.ds(m * 1024 + g * 128, 128), :] = ht[:, g * 128 : (g + 1) * 128]


def stage_pull(own, WR, C2, PP, PT):
    mask = iota((64, 128), 0) // 4 == own
    pull = jnp.where(mask, dot_nt(WR[64:128], C2[...]), 0.0)
    swap = iota((64, 64), 1) == (iota((64, 64), 0) ^ 4)
    PP[...] = dot(jnp.where(swap, 1.0, 0.0).astype(bf16), pull.astype(bf16)).astype(bf16)
    PT[...] = jnp.concatenate([pull, -pull], axis=0).T.astype(bf16)


def stage_grad_hidden(WR, C2, PT, GH):
    pt = PT[...]
    for m in range(4):
        cols = slice(m * 1024, (m + 1) * 1024)
        gh = (dot(pt, WR[:, cols]) + C2[:, cols].astype(f32)).astype(bf16)
        for g in range(8):
            GH[m, g * 128 : (g + 1) * 128, :] = gh[:, g * 128 : (g + 1) * 128]


def split_heads(part, m, G):
    part = part.astype(bf16)
    for g in range(8):
        G[g % 2, m * 4 + g // 2] = part[:, g * 128 : (g + 1) * 128]


def stage_projection(m, WR, HT, PP, LIFT, G):
    hidden = HT[pl.ds(m * 1024, 1024), :]
    LIFT[...] += dot(WR[:, pl.ds(pl.multiple_of(m * 1024, 1024), 1024)], hidden)
    split_heads(dot_nt(PP[...], hidden), m, G)


def stage_rotation(own, bias_sm, C2, LIFT, G, send):
    mask = iota((64, 128), 0) // 4 == own
    ridx = iota((8, 128), 0)
    shifts = []
    for b in range(8):
        a = jnp.zeros((8, 128), f32)
        for r in range(8):
            a = jnp.where(ridx == r, bias_sm[r % 4, (b * 8 + r) // 4], a)
        shifts.append(a)
    lift = LIFT[0:64] - LIFT[64:128] + jnp.concatenate(shifts, axis=0)
    lift = jnp.where(mask, lift, 0.0).astype(bf16)
    for m in range(4):
        split_heads(dot(lift, C2[:, m * 1024 : (m + 1) * 1024]), m, G)
        send(m)


def stage_bwd(m, KV, Q, P, GH, scale, DQ, SB, OWN):
    kt = KV[m, 0].T
    gh = GH[m]
    dp = dot_nt(KV[m, 1], gh)
    wl = P[m]
    w = wl.astype(f32)
    wd = w * dp
    delta = jnp.sum(wd, axis=0, keepdims=True)
    ds = (wd - w * delta).astype(bf16)
    dk = dot(ds, Q[m]) * scale
    dv = dot(wl, gh)
    for s in (1, 2):
        rows = slice(HALO - 128 * s, HALO - 128 * s + 128)
        SB[m, s - 1, 0] = dk[rows].astype(bf16)
        SB[m, s - 1, 1] = dv[rows].astype(bf16)
    OWN[m, 0] = dk[HALO:]
    OWN[m, 1] = dv[HALO:]
    dqt = dot(kt, ds) * scale
    for g in range(8):
        DQ[m * 8 + g] = dqt[:, g * 128 : (g + 1) * 128].T.astype(bf16)


REPS, CTXS, CHIPS = 16, 32, 16
FARTHEST_FIRST = sorted(range(1, REPS), key=lambda d: -min(d, REPS - d))
HALO = 256
VMEM_LIMIT = 60 << 20


def kernel(
    q_hbm, c_hbm, k_hbm, v_hbm, w_hbm, r_hbm, starts_hbm, owners_hbm, bias_sm,
    dq_hbm, dk_hbm, dv_hbm, gr_hbm, gp_hbm,
    q_in, c_in, k_in, v_in, w_in, r_in, starts_in, owners_in, in_sem,
    KV, Q, C2, WR, MB, P, HT, GH, PP, PT, LIFT,
    dq_out, dk_out, dv_out, grad_out, out_sem, DQ,
    halo_send, halo_recv, met,
    SB, RB, OWN, back_send, back_recv,
    G, R1, one_send, one_recv,
    S2, R2, two_send, two_recv,
    S3, R3, three_send, three_recv,
):
    rep = lax.axis_index("rep")
    ctx = lax.axis_index("ctx")
    chip = ctx // 2
    core = ctx % 2
    mate = ctx + 1 - 2 * core
    scale = 128 ** -0.5

    def there(x):
        return (rep, x)

    row_first = ctx * 128
    lanes = pl.ds(pl.multiple_of(row_first, 128), 128)
    loads = []
    for i, (src, dst) in enumerate((
        (k_hbm, k_in), (v_hbm, v_in),
        (starts_hbm.at[:, lanes], starts_in), (owners_hbm.at[:, lanes], owners_in),
        (q_hbm, q_in), (c_hbm, c_in), (w_hbm, w_in), (r_hbm, r_in),
    )):
        cp = pltpu.make_async_copy(src, dst, in_sem.at[i])
        cp.start()
        loads.append(cp)

    barrier = pltpu.get_barrier_semaphore()
    for d in [2 * d for d in FARTHEST_FIRST] + [1, CTXS - 1]:
        pl.semaphore_signal(barrier, inc=1, device_id=there((ctx + d) % CTXS), device_id_type=MESH)

    def along_z(d):
        return ((rep + d) % REPS, ctx)

    def greet_z(sem, d):
        for x in (d, REPS - d):
            pl.semaphore_signal(sem, inc=1, device_id=along_z(x), device_id_type=MESH)

    greet_z(barrier, 1)

    loads[0].wait()
    loads[1].wait()
    kk = jnp.swapaxes(k_in[...].astype(f32), 0, 1).astype(bf16)
    vv = jnp.swapaxes(v_in[...].astype(f32), 0, 1).astype(bf16)
    for m in range(4):
        KV[m, 0, HALO:] = kk[m]
        KV[m, 1, HALO:] = vv[m]
    pl.semaphore_wait(barrier, 2 + (CHIPS - 1) + 2)
    greet_z(met.at[0], 1)

    def far_copy(m):
        return pltpu.make_async_remote_copy(
            src_ref=KV.at[m, :, pl.ds(HALO, 128)],
            dst_ref=KV.at[m, :, pl.ds(0, 128)],
            send_sem=halo_send.at[m, 1],
            recv_sem=halo_recv.at[m, 1],
            device_id=there((ctx + 2) % CTXS),
            device_id_type=MESH,
        )

    def near_copy(m):
        return pltpu.make_async_remote_copy(
            src_ref=KV.at[m, :, pl.ds(pl.multiple_of(HALO * (1 - core), 128), 128)],
            dst_ref=KV.at[m, :, pl.ds(128, 128)],
            send_sem=halo_send.at[m, 0],
            recv_sem=halo_recv.at[m, 0],
            device_id=there(mate),
            device_id_type=MESH,
        )

    for m in range(4):
        far_copy(m).start()

    @pl.when(core == 0)
    def _():
        for m in range(4):
            near_copy(m).start()

    for cp in loads[2:]:
        cp.wait()
    stage_prep(q_in, c_in, w_in, r_in, Q, C2, WR)
    own = owners_in[...]
    stage_mask(starts_in[...], row_first, MB)
    stage_pull(own, WR, C2, PP, PT)
    LIFT[...] = jnp.zeros_like(LIFT)
    pl.semaphore_wait(met.at[0], 2)
    greet_z(met.at[1], 2)

    def one_copy(p, m):
        return pltpu.make_async_remote_copy(
            src_ref=G.at[p, 1 - core, pl.ds(4 * m, 4)],
            dst_ref=R1.at[p, pl.ds(4 * m, 4)],
            send_sem=one_send.at[p, m],
            recv_sem=one_recv.at[p, m],
            device_id=there(mate),
            device_id_type=MESH,
        )

    def two_copy(p, d):
        return pltpu.make_async_remote_copy(
            src_ref=S2.at[p, (chip + d) % CHIPS],
            dst_ref=R2.at[p, d],
            send_sem=two_send.at[p, d],
            recv_sem=two_recv.at[p, d],
            device_id=there((ctx + 2 * d) % CTXS),
            device_id_type=MESH,
        )

    def pair_sum(p, m):
        one_copy(p, m).wait_recv()
        part = pl.ds(4 * m, 4)
        S2[p, part] = (G[p, core, part].astype(f32) + R1[p, part].astype(f32)).astype(bf16)
        for i in range(4):
            d = (4 * m + i + CHIPS - chip) % CHIPS

            @pl.when(d > 0)
            def _():
                two_copy(p, d).start()

    def chip_sum(p):
        total = S2[p, chip].astype(f32)
        for d in range(1, CHIPS):
            two_copy(p, d).wait_recv()
            total = total + R2[p, d].astype(f32)
        return total

    def spread():
        proj, rot = chip_sum(1), chip_sum(0)
        upper = iota((8, 128), 0) < 4
        for t in range(0, REPS, 2):
            a, c = rot[4 * t : 4 * t + 8], proj[4 * t : 4 * t + 8]
            S3[t] = jnp.where(upper, a, c)
            S3[t + 1] = jnp.where(upper, c, a)
        pl.semaphore_wait(met.at[2], 2)
        for d in FARTHEST_FIRST:
            three_copy(d).start()

    def three_copy(d):
        return pltpu.make_async_remote_copy(
            src_ref=S3.at[(rep + d) % REPS],
            dst_ref=R3.at[d],
            send_sem=three_send.at[d],
            recv_sem=three_recv.at[d],
            device_id=along_z(d),
            device_id_type=MESH,
        )

    def fwd(m, carry):
        far_copy(m).wait_recv()

        @pl.when(core == 1)
        def _():
            near_copy(m).start()

        near_copy(m).wait_recv()
        stage_fwd(m, KV, Q, MB, P, HT, scale)
        stage_projection(m, WR, HT, PP, LIFT, G.at[1])
        one_copy(1, m).start()

        return carry

    lax.fori_loop(0, 4, fwd, 0)
    pl.semaphore_wait(met.at[1], 2)
    greet_z(met.at[2], 4)

    def back_copy(m, s):
        return pltpu.make_async_remote_copy(
            src_ref=SB.at[m, s - 1],
            dst_ref=RB.at[m, s - 1],
            send_sem=back_send.at[m, s - 1],
            recv_sem=back_recv.at[m, s - 1],
            device_id=there((ctx + CTXS - s) % CTXS),
            device_id_type=MESH,
        )

    for m in range(3):
        pair_sum(1, m)
    stage_rotation(own, bias_sm, C2, LIFT, G.at[0], lambda m: one_copy(0, m).start())
    pair_sum(1, 3)
    stage_grad_hidden(WR, C2, PT, GH)
    for m in range(4):
        pair_sum(0, m)

    def bwd(m, carry):
        stage_bwd(m, KV, Q, P, GH, scale, DQ, SB, OWN)

        for s in (1, 2):
            back_copy(m, s).start()
        return carry

    lax.fori_loop(0, 4, bwd, 0)
    spread()

    stores = []
    for m in range(4):
        heads = slice(8 * m, 8 * m + 8)
        dq_out[:, heads, :] = jnp.swapaxes(DQ[heads], 0, 1)
        cp = pltpu.make_async_copy(dq_out.at[:, heads], dq_hbm.at[:, heads], out_sem.at[m])
        cp.start()
        stores.append(cp)

    for m in range(4):
        for s in (1, 2):
            back_copy(m, s).wait_recv()
    total = OWN[...] + RB[:, 0].astype(f32) + RB[:, 1].astype(f32)
    dk_out[...] = jnp.swapaxes(total[:, 0], 0, 1).astype(bf16)
    dv_out[...] = jnp.swapaxes(total[:, 1], 0, 1).astype(bf16)
    for i, (src, dst) in enumerate(((dk_out, dk_hbm), (dv_out, dv_hbm))):
        cp = pltpu.make_async_copy(src, dst, out_sem.at[6 + i])
        cp.start()
        stores.append(cp)

    mine = S3[rep]
    for d in range(1, REPS):
        three_copy(d).wait_recv()
        mine = mine + R3[d]
    odd = rep % 2 == 1
    low, high = mine[0:4], mine[4:8]
    proj = jnp.where(odd, low, high)
    grad_out[0] = jnp.where(odd, high, low) - proj
    grad_out[1] = proj
    for i, dst in enumerate((gr_hbm, gp_hbm)):
        cp = pltpu.make_async_copy(grad_out.at[i], dst, out_sem.at[4 + i])
        cp.start()
        stores.append(cp)

    for m in range(4):
        one_copy(0, m).wait_send()
        one_copy(1, m).wait_send()
        far_copy(m).wait_send()
        near_copy(m).wait_send()
        for s in (1, 2):
            back_copy(m, s).wait_send()
    for d in range(1, CHIPS):
        two_copy(0, d).wait_send()
        two_copy(1, d).wait_send()
    for d in range(1, REPS):
        three_copy(d).wait_send()
    for cp in stores:
        cp.wait()


def finish(*refs):
    srcs, dsts, bufs, sems = refs[:5], refs[5:10], refs[10:15], refs[15]
    moves = [(srcs[i], bufs[i], dsts[i]) for i in range(1, 5)]
    for i in range(4):
        rows = pl.ds(32 * i, 32)
        moves.append((srcs[0].at[rows], bufs[0].at[rows], dsts[0].at[rows]))
    loads, stores = [], []
    for i, (src, buf, dst) in enumerate(moves):
        loads.append(pltpu.make_async_copy(src, buf, sems.at[0, i]))
        stores.append(pltpu.make_async_copy(buf, dst, sems.at[1, i]))
        loads[i].start()
    for load, store in zip(loads, stores):
        load.wait()
        store.start()
    for store in stores:
        store.wait()


def on_device(
    query_rows, key_rows, value_matrix, cotangent, rotation, projection, shift_bias,
    doc_starts, tenant_ids,
):
    smem = pl.BlockSpec(memory_space=pltpu.SMEM)
    hbm = pl.BlockSpec(memory_space=pltpu.HBM)
    dma = pltpu.SemaphoreType.DMA
    rows = (128, 32, 128)
    kv_rows = (128, 4, 128)
    out_shape = (
        jax.ShapeDtypeStruct(rows, bf16),
        jax.ShapeDtypeStruct(kv_rows, bf16),
        jax.ShapeDtypeStruct(kv_rows, bf16),
        jax.ShapeDtypeStruct((4, 128), f32),
        jax.ShapeDtypeStruct((4, 128), f32),
    )
    out = pl.pallas_call(
        kernel,
        out_shape=out_shape,
        in_specs=[hbm] * 8 + [smem],
        out_specs=(hbm,) * 5,
        scratch_shapes=[
            pltpu.VMEM(rows, bf16), pltpu.VMEM(rows, bf16),
            pltpu.VMEM((128, 4, 128), bf16), pltpu.VMEM((128, 4, 128), bf16),
            pltpu.VMEM((64, 32, 128), bf16), pltpu.VMEM((64, 32, 128), bf16),
            pltpu.VMEM((1, 128), jnp.int32), pltpu.VMEM((1, 128), jnp.int32),
            dma((8,)),
            pltpu.VMEM((4, 2, 384, 128), bf16),
            pltpu.VMEM((4, 1024, 128), bf16),
            pltpu.VMEM((128, 4096), bf16),
            pltpu.VMEM((128, 4096), bf16),
            pltpu.VMEM((384, 128), f32),
            pltpu.VMEM((4, 384, 1024), bf16),
            pltpu.VMEM((4096, 128), bf16),
            pltpu.VMEM((4, 1024, 128), bf16),
            pltpu.VMEM((64, 128), bf16),
            pltpu.VMEM((128, 128), bf16),
            pltpu.VMEM((128, 128), f32),
            pltpu.VMEM(rows, bf16), pltpu.VMEM((128, 4, 128), bf16), pltpu.VMEM((128, 4, 128), bf16),
            pltpu.VMEM((2, 4, 128), f32), dma((8,)),
            pltpu.VMEM((32, 128, 128), bf16),
            dma((4, 2)), dma((4, 2)), pltpu.SemaphoreType.REGULAR((3,)),
            pltpu.VMEM((4, 2, 2, 128, 128), bf16),
            pltpu.VMEM((4, 2, 2, 128, 128), bf16),
            pltpu.VMEM((4, 2, 128, 128), f32),
            dma((4, 2)), dma((4, 2)),
            pltpu.VMEM((2, 2, CHIPS, 64, 128), bf16),
            pltpu.VMEM((2, CHIPS, 64, 128), bf16),
            dma((2, 4)), dma((2, 4)),
            pltpu.VMEM((2, CHIPS, 64, 128), bf16),
            pltpu.VMEM((2, CHIPS, 64, 128), bf16),
            dma((2, CHIPS)), dma((2, CHIPS)),
            pltpu.VMEM((REPS, 8, 128), f32),
            pltpu.VMEM((REPS, 8, 128), f32),
            dma((REPS,)), dma((REPS,)),
        ],
        compiler_params=pltpu.CompilerParams(
            collective_id=0, has_side_effects=True, vmem_limit_bytes=VMEM_LIMIT
        ),
        name="steered_attention_backward",
    )(
        query_rows[0], cotangent[0], key_rows[0], value_matrix[0],
        projection.reshape(64, 32, 128), rotation.reshape(64, 32, 128),
        doc_starts, tenant_ids, shift_bias.T,
    )
    dq, dk, dv, gr, gp = pl.pallas_call(
        finish,
        out_shape=out_shape,
        in_specs=[hbm] * 5,
        out_specs=(hbm,) * 5,
        scratch_shapes=[pltpu.VMEM(s.shape, s.dtype) for s in out_shape] + [dma((2, 8))],
        compiler_params=pltpu.CompilerParams(vmem_limit_bytes=VMEM_LIMIT),
        name="finish",
    )(*out)
    return dq[None], dk[None], dv[None], gr.reshape(1, 4, 1, 128), gp.reshape(1, 4, 1, 128)


def solution(mesh):
    row = P_("rep", "ctx", None, None)
    in_specs = (row, row, row, row, P_(), P_(), P_(), P_("rep", None), P_("rep", None))
    grads = P_("rep", None, "ctx", None)
    return jax.shard_map(
        on_device, mesh=mesh, in_specs=in_specs, out_specs=(row, row, row, grads, grads),
        check_vma=False,
    )
```
